32 devices in a mesh: segment: 4 (over y, x), chan: 8 (over z, core).
Axes of the slice: x: 2, y: 2, z: 4, core: 2. Of those that a mesh axis runs over, the one named last changes fastest.
Arguments:
- resident: float32 [4, 1280, 512], P('segment', 'chan'), may hold values from -6 to 6
- held_skip: float32 [4, 1280, 512], P('segment', 'chan'), may hold values from -6 to 6
- fresh: float32 [2, 1280, 512], P(None, 'chan'), may hold values from -6 to 6
- first_weight: float32 [4, 1280, 11520], P('segment', 'chan'), may hold values from -0.0546875 to 0.0546875
- second_weight: float32 [4, 1280, 11520], P('segment', 'chan'), may hold values from -0.0546875 to 0.0546875
Outputs:
- last_outputs: float32 [4, 1280, 512], P('segment', 'chan')
The draws below stay inside these ranges and needn't reach their ends.
All inputs are finite; a program needn't handle non-finite values.
Results may differ from the reference program's by a relative error of at most 0.0001.
Values sent between devices are 32-bit elements; how exact they have to be, the bound alone decides.
A program may use at most 128 MiB of HBM per device.

```python
import jax
import jax.numpy as jnp
from jax import lax

C = 1280
ROWS = 16
COLS = 32
TICKS = 3
P_SIZE = 512
SECTIONS = 4


def block_levels(key, dims, shards, least, high):
    def one(position, parts):
        draws = jax.random.uniform(jax.random.fold_in(jax.random.fold_in(key, 6), position), (parts,), jnp.float32, least / len(shards), high / len(shards))
        return jnp.repeat(jnp.exp(draws), dims[position] // parts).reshape((-1,) + (1,) * (len(dims) - position - 1))

    factor_of = one(*shards[0])
    for cut in shards[1:]:
        factor_of = factor_of * one(*cut)
    return factor_of


def scatter_about(rng, dims, scale, most, pieces=(), dtype=jnp.bfloat16):
    entries = scale * jax.random.normal(rng, dims, jnp.float32)
    if pieces:
        entries = entries * block_levels(rng, dims, pieces, -0.22, 0.18)
    return jnp.clip(entries, -most, most).astype(dtype)


def setup_inputs(seed: int = 0) -> dict:
    streams_of = jax.random.split(jax.random.key(seed), 6)
    return {
        "resident": scatter_about(streams_of[0], (SECTIONS, C, P_SIZE), 1.0, 6.0, ((0, 4), (1, 8)), jnp.float32),
        "held_skip": scatter_about(streams_of[1], (SECTIONS, C, P_SIZE), 1.0, 6.0, ((0, 4), (1, 8)), jnp.float32),
        "fresh": scatter_about(streams_of[2], (TICKS - 1, C, P_SIZE), 1.0, 6.0, ((1, 8),), jnp.float32),
        "first_weight": scatter_about(streams_of[3], (SECTIONS, C, 9 * C), (9 * C) ** -0.5, 0.0546875, ((0, 4), (1, 8)), jnp.float32),
        "second_weight": scatter_about(streams_of[4], (SECTIONS, C, 9 * C), (9 * C) ** -0.5, 0.0546875, ((0, 4), (1, 8)), jnp.float32),
    }


def tap_shift(x, dy, dx):
    grid = x.reshape(x.shape[:-1] + (ROWS, COLS))
    padded = jnp.pad(grid, [(0, 0)] * (grid.ndim - 2) + [(1, 1), (1, 1)])
    moved = padded[..., 1 + dy:1 + dy + ROWS, 1 + dx:1 + dx + COLS]
    return moved.reshape(x.shape)


def convolve(weight, field):
    shifted = jnp.stack([tap_shift(field, dy, dx) for dy in (-1, 0, 1) for dx in (-1, 0, 1)])
    return jnp.dot(weight, shifted.reshape(9 * C, ROWS * COLS), precision=lax.Precision.HIGHEST, preferred_element_type=jnp.float32)


def section(inputs):
    w_first, w_second, field, skip, encoder = inputs
    first = convolve(w_first, field)
    operand = jnp.where(encoder, jax.nn.silu(first), skip)
    second = convolve(w_second, operand)
    return jnp.where(encoder, field + second, jax.nn.silu(first + second))


def reference(resident, held_skip, fresh, first_weight, second_weight):
    encoder = jnp.arange(SECTIONS) < SECTIONS // 2
    state = resident
    skip = held_skip
    outputs = resident
    for tick in range(TICKS):
        outputs = lax.map(section, (first_weight, second_weight, state, skip, encoder))
        if tick < TICKS - 1:
            state = jnp.concatenate([fresh[tick][None], outputs[:-1]], axis=0)
            skip = jnp.where(encoder[:, None, None], skip, outputs[::-1])
    return outputs
```

```python
import functools

import jax
import jax.numpy as jnp
from jax import lax
from jax.experimental import pallas as pl
from jax.experimental.pallas import tpu as pltpu
from jax.sharding import PartitionSpec as P

ROWS = 16
COLS = 32
MESH = pl.DeviceIdType.MESH
HALVES = 2
PIECES = 2
CHUNKS = HALVES * PIECES
UNITS = 8
OWN_UNITS = 6
PARTS = ((0, UNITS // 2), (UNITS // 2, OWN_UNITS), (OWN_UNITS, UNITS))


def silu(v):
    return v / (1.0 + jnp.exp(-v))


def block_of(rows):
    for size in (32, 40, 16):
        if rows % size == 0:
            return size
    return 8


def first_decoder_tick(segments, ticks):
    return max(0, ticks - segments // 2)


def kernel(
    segments, n, ticks,
    resident, held_skip, fresh, first_weight, second_weight, out_ref,
    stage, wv, g, operand, acc, passed_out,
    w_sem, recv_sem, swap_sem, partner_sem, z_sem, y_sem, pass_sem,
):
    seg = lax.axis_index("segment")
    me = lax.axis_index("chan")
    place = me // 2
    core = me % 2
    partner = me + 1 - 2 * core
    length = n // 2
    half = segments // 2
    encoder = seg < half
    decoder = jnp.logical_not(encoder)
    first_tick = first_decoder_tick(segments, ticks)
    merge = first_tick >= 1
    merged = (seg == half) & merge
    rows, positions = resident.shape
    part_positions = positions // HALVES
    piece = positions // CHUNKS
    width = 2 * rows
    channels = length * width
    blk = block_of(rows)
    split_blk = 32 if rows % 32 == 0 else rows
    up = jnp.minimum(me + 2, n - 1)
    down = jnp.maximum(me - 2, 0)
    has_up = place < length - 1
    has_down = place > 0
    twin = jnp.where(encoder, seg + half, seg - half)

    def load(conv, tap, slot):
        source = (first_weight, second_weight)[conv]
        columns = pl.ds(pl.multiple_of(tap * channels, 128), channels)
        return pltpu.make_async_copy(source.at[0, :, columns], stage.at[slot], w_sem.at[slot])

    def store_split(conv, tap, value_of):
        def some_rows(i, _):
            start = i * split_blk
            if split_blk != rows:
                start = pl.multiple_of(start, 16)
            spot = pl.ds(pl.multiple_of(tap * rows + start, 16), split_blk)
            for q in range(length):
                value = value_of(pl.ds(start, split_blk), slice(q * width, (q + 1) * width))
                high = value.astype(jnp.bfloat16)
                low = (value - high.astype(jnp.float32)).astype(jnp.bfloat16)
                wv[conv, q, spot, 0:width] = high
                wv[conv, q, spot, width : 2 * width] = low
                wv[conv, q, spot, 2 * width : 3 * width] = high
            return 0
        lax.fori_loop(0, rows // split_blk, some_rows, 0)

    depth = 4

    def start_first_loads():
        @pl.when(jnp.logical_not(merged))
        def _():
            def one(tap, _):
                load(0, tap, tap).start()
                return 0
            lax.fori_loop(0, 9, one, 0)

        if merge:
            @pl.when(merged)
            def _():
                for tap in range(depth):
                    load(0, tap, tap).start()
                    load(1, tap, depth + tap).start()

    def split_taps(conv, low, high):
        def one(tap, _):
            load(0, 0, tap).wait()
            store_split(conv, tap, lambda r, c: stage[tap, r, c])
            return 0
        lax.fori_loop(low, high, one, 0)

    def reload_taps(low, high):
        def one(tap, _):
            load(1, tap, tap).start()
            return 0
        lax.fori_loop(low, high, one, 0)

    def split_merged(low, high):
        def one(tap, _):
            a = tap % depth
            load(0, 0, a).wait()
            load(1, 0, depth + a).wait()
            store_split(0, tap, lambda r, c: stage[a, r, c] + stage[depth + a, r, c])

            @pl.when(tap + depth < 9)
            def _():
                load(0, tap + depth, a).start()
                load(1, tap + depth, depth + a).start()
            return 0
        lax.fori_loop(low, high, one, 0)

    start_first_loads()

    barrier = pltpu.get_barrier_semaphore()

    def greet(cond, segment, chan):
        @pl.when(cond)
        def _():
            pl.semaphore_signal(barrier, inc=1, device_id=(segment, chan), device_id_type=MESH)
        return jnp.where(cond, 1, 0)

    def kept(s):
        return jnp.clip(s, 0, segments - 1)

    greeted = greet(has_down, seg, down)
    greeted += greet(has_up, seg, up)
    greeted += greet(seg >= 0, seg, partner)
    greeted += greet(seg > 0, kept(seg - 1), me)
    greeted += greet(seg < segments - 1, kept(seg + 1), me)
    greeted += greet(seg >= 0, segments - 1 - seg, me)
    greeted += greet(seg >= 0, twin, me)
    greeted += greet(seg + 1 < half, kept(seg + 1 + half), me)
    greeted += greet(seg >= half + 1, kept(seg - 1 - half), me)

    def encoder_slot(t, kind):
        return 2 * t + kind

    def decoder_slot(t, kind):
        return 2 * ticks + 2 * jnp.maximum(t - first_tick, 0) + kind

    def decoder_active(s, t):
        return s + (ticks - 1 - t) <= segments - 1

    shared = (segments + half) // 2
    shares = seg == shared
    if (segments + half) % 2:
        shares = seg < 0

    unit = CHUNKS * rows // UNITS

    def units_of(u, count):
        return pl.ds(u * unit, count * unit)

    def copy(k, q, u, count, sem, target_seg, target):
        return pltpu.make_async_remote_copy(
            src_ref=g.at[k, core, q, units_of(u, count)],
            dst_ref=g.at[k, core, q, units_of(u, count)],
            send_sem=sem,
            recv_sem=recv_sem.at[k, q, u],
            device_id=(target_seg, target),
            device_id_type=MESH,
        )

    def swap(k, parity, q, part):
        low, high = PARTS[part]
        return pltpu.make_async_remote_copy(
            src_ref=g.at[k, parity, q, units_of(low, high - low)],
            dst_ref=g.at[k, parity, q, units_of(low, high - low)],
            send_sem=partner_sem.at[k],
            recv_sem=swap_sem.at[k, q, part],
            device_id=(seg, partner),
            device_id_type=MESH,
        )

    def along(k, q, u, way):
        return copy(k, q, u, 1, z_sem.at[k, way, q], seg, (down, up)[way])

    def across(k, q, u):
        return copy(k, q, u, 1, y_sem.at[k, q], twin, me)

    def arrived(k, q, u):
        copy(k, q, u, 1, y_sem.at[k, q], twin, me).wait_recv()

    def both_ways(k, u):
        @pl.when(has_up)
        def _():
            along(k, place, u, 1).start()

        @pl.when(has_down)
        def _():
            along(k, place, u, 0).start()

    def onward(k, q, u):
        @pl.when((q > place) & has_down)
        def _():
            along(k, q, u, 0).start()

        @pl.when((q < place) & has_up)
        def _():
            along(k, q, u, 1).start()

    def swap_after(k, q, u):
        for part, (low, high) in enumerate(PARTS):
            if u == high - 1:
                swap(k, core, q, part).start()

    near = jnp.minimum(place, length - 1 - place)
    inner = jnp.where(place < length // 2, 1, -1)

    def source_of(i):
        paired = i < 2 * near
        d = jnp.where(paired, i // 2 + 1, i - near + 1)
        way = jnp.where(paired & (i % 2 == 1), -inner, inner)
        return place + way * d

    def multiply(k, w, q, h):
        for i in range(2):
            for p in range(PIECES):
                part = g[k, i, q, pl.ds((PIECES * h + p) * rows, rows)]
                high = part.astype(jnp.bfloat16)
                low = (part - high.astype(jnp.float32)).astype(jnp.bfloat16)
                cut = slice(p * piece, (p + 1) * piece)
                operand[i * rows : (i + 1) * rows, cut] = high
                operand[width + i * rows : width + (i + 1) * rows, cut] = high
                operand[2 * width + i * rows : 2 * width + (i + 1) * rows, cut] = low
        acc[h] += jnp.dot(wv[w, q], operand[...], preferred_element_type=jnp.float32)

    spot = lax.broadcasted_iota(jnp.int32, (blk, positions), 1)
    column = spot % COLS

    def placed(start):
        total = None
        for dx in (-1, 0, 1):
            column_sum = None
            for dy in (-1, 0, 1):
                tap = 3 * (dy + 1) + dx + 1
                at = pl.ds(pl.multiple_of(tap * rows + start, 8), blk)
                part = jnp.concatenate([acc[h, at, :] for h in range(HALVES)], axis=1)
                if dy:
                    part = pltpu.roll(part, (-dy * COLS) % positions, 1)
                    source = spot + dy * COLS
                    part = jnp.where((source >= 0) & (source < positions), part, 0.0)
                column_sum = part if column_sum is None else column_sum + part
            if dx:
                column_sum = pltpu.roll(column_sum, (-dx) % positions, 1)
                source = column + dx
                column_sum = jnp.where((source >= 0) & (source < COLS), column_sum, 0.0)
            total = column_sum if total is None else total + column_sum
        return total

    def over_rows(action):
        def one(i, _):
            start = pl.multiple_of(i * blk, 8)
            action(start, pl.ds(start, blk))
            return 0
        lax.fori_loop(0, rows // blk, one, 0)

    def cut_of(c):
        return slice(c * piece, (c + 1) * piece)

    def rows_at(c, start=0, count=None):
        return pl.ds(c * rows + start, rows if count is None else count)

    def fill(k, source):
        for c in range(CHUNKS):
            g[k, core, place, rows_at(c)] = source[:, cut_of(c)]

    @pl.when(encoder)
    def _():
        fill(0, resident)

    if first_tick == 0:
        @pl.when(decoder)
        def _():
            fill(2 * ticks, resident)
            fill(2 * ticks + 1, held_skip)

    @pl.when((seg == 0) | (seg == half))
    def _():
        for t in range(1, ticks):
            fill(2 * t, fresh.at[t - 1])

    pl.semaphore_wait(barrier, greeted)

    def drain_along(k, low, high):
        def one(q, _):
            @pl.when(has_up & (q <= place))
            def _():
                copy(k, q, low, high - low, z_sem.at[k, 1, q], seg, up).wait_send()

            @pl.when(has_down & (q >= place))
            def _():
                copy(k, q, low, high - low, z_sem.at[k, 0, q], seg, down).wait_send()
            return 0
        lax.fori_loop(0, length, one, 0)

    def drain_partner(k):
        pltpu.make_async_remote_copy(
            src_ref=g.at[k, core], dst_ref=g.at[k, core],
            send_sem=partner_sem.at[k], recv_sem=swap_sem.at[k, 0, 0],
            device_id=(seg, partner), device_id_type=MESH,
        ).wait_send()

    def drain_across(k, q, low, high):
        copy(k, q, low, high - low, y_sem.at[k, q], twin, me).wait_send()

    def facts_of(idx):
        t = idx // 2
        kind = idx % 2
        skip_held = shares & (kind == 1) & (t > 0)
        k = jnp.where(
            encoder,
            encoder_slot(t, kind),
            jnp.where(skip_held, encoder_slot(t, 0), decoder_slot(t, kind)),
        )
        active = encoder | (decoder_active(seg, t) & jnp.logical_not(merged & (kind == 1)))
        lifts = encoder & ((kind == 1) | (t == 0))
        lends = encoder & (twin == shared) & (kind == 0) & (t > 0) & decoder_active(twin, t)
        if (segments + half) % 2:
            lends = lends & (seg < 0)
        return t, kind, k, active, lifts, lends, skip_held

    def drain(idx):
        t, kind, k, active, lifts, lends, skip_held = facts_of(idx)
        relayed = encoder_slot(t, kind)

        @pl.when(active)
        def _():
            drain_partner(k)

            @pl.when(encoder)
            def _():
                drain_along(k, 0, OWN_UNITS)

                @pl.when(lifts)
                def _():
                    drain_across(k, place, OWN_UNITS, UNITS)

                @pl.when(lends)
                def _():
                    def one(q, _):
                        drain_across(k, q, 0, OWN_UNITS)
                        return 0
                    lax.fori_loop(0, length, one, 0)

            @pl.when(decoder & jnp.logical_not(skip_held))
            def _():
                drain_along(k, 0, UNITS)

        @pl.when(decoder)
        def _():
            drain_along(relayed, OWN_UNITS, UNITS)

            def one(q, _):
                @pl.when(q != place)
                def _():
                    drain_across(relayed, q, OWN_UNITS, UNITS)
                return 0
            lax.fori_loop(0, length, one, 0)

    others = length - 1
    slots = 2 * length
    third = slots - 4

    at_end = near == 0

    def event_of(e):
        m = (e + 1) // 2
        h = jnp.where(e == 0, 0, jnp.where(e == 2 * others - 1, 1, (e + 1) % 2))
        i = jnp.where(e == 0, 0, jnp.where(e % 2 == 1, jnp.minimum(m, others - 1), e // 2 - 1))
        return jnp.where(at_end, e // 2, i), jnp.where(at_end, e % 2, h)

    def one_stage(idx, _):
        t, kind, k, active, lifts, lends, skip_held = facts_of(idx)
        relayed = encoder_slot(t, kind)
        local = jnp.where(encoder, (kind == 1) | (t == 0) | (seg == 0), t == 0)
        ahead = (seg == 0) & (kind == 0) & (t > 0)

        @pl.when(decoder)
        def _():
            for u in range(OWN_UNITS, UNITS):
                @pl.when(jnp.logical_not((seg == half) & (kind == 0) & (t > 0)))
                def _():
                    arrived(relayed, place, u)
                both_ways(relayed, u)

        @pl.when(active)
        def _():
            for u in range(UNITS):
                if u < OWN_UNITS:
                    @pl.when(jnp.logical_not(local))
                    def _():
                        arrived(k, place, u)

                    @pl.when(jnp.logical_not(ahead | skip_held))
                    def _():
                        both_ways(k, u)

                    @pl.when(lends)
                    def _():
                        across(k, place, u).start()
                else:
                    @pl.when(jnp.logical_not(local | skip_held))
                    def _():
                        arrived(k, place, u)

                    @pl.when(decoder & jnp.logical_not(skip_held))
                    def _():
                        both_ways(k, u)

                    @pl.when(lifts)
                    def _():
                        across(k, place, u).start()
                swap_after(k, place, u)

            @pl.when(encoder | (kind == 0))
            def _():
                acc[...] = jnp.zeros_like(acc)

        @pl.when(idx > 0)
        def _():
            drain(idx - 1)

        @pl.when(encoder & (idx == 0))
        def _():
            split_taps(0, 0, 9)
            reload_taps(0, 9)

        def one_slot(s, _):
            @pl.when(decoder & (s >= 1) & (s < length))
            def _():
                q = source_of(s - 1)
                for u in range(OWN_UNITS, UNITS):
                    arrived(relayed, q, u)
                    onward(relayed, q, u)
                    across(relayed, q, u).start()

            e, part = event_of(jnp.maximum(s - 1, 0))
            gathers = active & (s >= 1) & (s <= 2 * others)

            @pl.when(gathers & (part == 0))
            def _():
                q = source_of(e)
                for u in range(OWN_UNITS):
                    arrived(k, q, u)

                    @pl.when(jnp.logical_not(skip_held))
                    def _():
                        onward(k, q, u)

                    @pl.when(lends)
                    def _():
                        across(k, q, u).start()
                    swap_after(k, q, u)

            @pl.when(gathers & (part == 1))
            def _():
                q = source_of(e)
                for u in range(OWN_UNITS, UNITS):
                    @pl.when(jnp.logical_not(skip_held))
                    def _():
                        arrived(k, q, u)

                    @pl.when(decoder & jnp.logical_not(skip_held))
                    def _():
                        onward(k, q, u)
                    swap_after(k, q, u)

            @pl.when((seg == 0) & (kind == 1) & (t < ticks - 1) & (s == 2 * others - 1))
            def _():
                for u in range(OWN_UNITS):
                    both_ways(k + 1, u)

            @pl.when((s >= third) & (s < third + 3))
            def _():
                low = 3 * (s - third)

                @pl.when(encoder & (idx == 0))
                def _():
                    split_taps(1, low, low + 3)

                @pl.when(decoder & jnp.logical_not(merged) & (idx == 0))
                def _():
                    split_taps(0, low, low + 3)
                    reload_taps(low, low + 3)

                @pl.when(decoder & jnp.logical_not(merged) & (idx == 1))
                def _():
                    split_taps(1, low, low + 3)

                if merge:
                    @pl.when(merged & (idx == 0))
                    def _():
                        split_merged(low, low + 3)

            @pl.when(active)
            def _():
                i, h = event_of(jnp.maximum(s - 2, 0))
                q = jnp.where(s < 2, place, source_of(i))
                h = jnp.where(s < 2, s, h)

                @pl.when(h == 0)
                def _():
                    swap(k, 1 - core, q, 0).wait_recv()

                @pl.when(h == 1)
                def _():
                    swap(k, 1 - core, q, 1).wait_recv()
                    swap(k, 1 - core, q, 2).wait_recv()
                multiply(k, kind, q, h)
            return 0
        lax.fori_loop(0, slots, one_slot, 0)

        def after(start, rows_of):
            value = placed(start)

            def put(parts):
                @pl.when(t == ticks - 1)
                def _():
                    for c in range(CHUNKS):
                        out_ref[rows_of, cut_of(c)] = parts[c]

                @pl.when(t < ticks - 1)
                def _():
                    for c in range(CHUNKS):
                        passed_out[jnp.minimum(t, ticks - 2), rows_at(c, start, blk), :] = parts[c]

            @pl.when(encoder & (kind == 0))
            def _():
                result = silu(value)
                for c in range(CHUNKS):
                    g[k + 1, core, place, rows_at(c, start, blk), :] = result[:, cut_of(c)]

            @pl.when(encoder & (kind == 1))
            def _():
                put([
                    g[k - 1, core, place, rows_at(c, start, blk), :] + value[:, cut_of(c)]
                    for c in range(CHUNKS)
                ])

            @pl.when(decoder)
            def _():
                result = silu(value)
                put([result[:, cut_of(c)] for c in range(CHUNKS)])

        ends = active & ((kind == 1) | merged)

        @pl.when(encoder | ends)
        def _():
            over_rows(after)

        @pl.when(ends & (t < ticks - 1))
        def _():
            give_all(t, True)
        return 0

    def give(t, kind, u, count):
        into_encoder = seg + 1 < half
        slot = (
            jnp.where(into_encoder, encoder_slot(t + 1, 0), decoder_slot(t + 1, 0)),
            encoder_slot(t + 1, 0),
            decoder_slot(t + 1, 1),
        )[kind]
        target = (kept(seg + 1), kept(seg + 1 + half), segments - 1 - seg)[kind]
        return pltpu.make_async_remote_copy(
            src_ref=passed_out.at[t, units_of(u, count)],
            dst_ref=g.at[slot, core, place, units_of(u, count)],
            send_sem=pass_sem.at[t, kind],
            recv_sem=recv_sem.at[slot, place, u],
            device_id=(target, me),
            device_id_type=MESH,
        )

    def give_all(t, starting):
        next_in = (seg + 1 < half) | ((seg < segments - 1) & decoder_active(seg + 1, t + 1))
        helper = seg + 1 < half
        mirror = segments - 1 - seg
        skip = encoder & decoder_active(mirror, t + 1)
        if merge:
            skip = skip & (mirror != half)
        if (segments + half) % 2 == 0:
            skip = skip & (mirror != shared)
        if starting:
            @pl.when(helper)
            def _():
                for u in range(OWN_UNITS, UNITS):
                    give(t, 1, u, 1).start()

            @pl.when(next_in)
            def _():
                for u in range(OWN_UNITS):
                    give(t, 0, u, 1).start()

            @pl.when(next_in)
            def _():
                for u in range(OWN_UNITS, UNITS):
                    give(t, 0, u, 1).start()

            @pl.when(skip)
            def _():
                for u in range(UNITS):
                    give(t, 2, u, 1).start()
        else:
            @pl.when(next_in)
            def _():
                give(t, 0, 0, UNITS).wait_send()

            @pl.when(helper)
            def _():
                give(t, 1, OWN_UNITS, UNITS - OWN_UNITS).wait_send()

            @pl.when(skip)
            def _():
                give(t, 2, 0, UNITS).wait_send()

    lax.fori_loop(0, 2 * ticks, one_stage, 0)
    drain(2 * ticks - 1)

    for t in range(ticks - 1):
        @pl.when(encoder | decoder_active(seg, t))
        def _():
            give_all(t, False)


def body(segments, n, resident, held_skip, fresh, first_weight, second_weight):
    ticks = fresh.shape[0] + 1
    rows, positions = resident.shape[1:]
    length = n // 2
    width = 2 * rows
    slots = 2 * ticks + 2 * (ticks - first_decoder_tick(segments, ticks))
    vmem = pl.BlockSpec(memory_space=pltpu.VMEM)
    anywhere = pl.BlockSpec(memory_space=pl.ANY)
    out = pl.pallas_call(
        functools.partial(kernel, segments, n, ticks),
        out_shape=jax.ShapeDtypeStruct((rows, positions), jnp.float32),
        in_specs=[vmem, vmem, vmem, anywhere, anywhere],
        out_specs=vmem,
        scratch_shapes=[
            pltpu.VMEM((9, rows, length * width), jnp.float32),
            pltpu.VMEM((2, length, 9 * rows, 3 * width), jnp.bfloat16),
            pltpu.VMEM((slots, 2, length, CHUNKS * rows, positions // CHUNKS), jnp.float32),
            pltpu.VMEM((3 * width, positions // HALVES), jnp.bfloat16),
            pltpu.VMEM((HALVES, 9 * rows, positions // HALVES), jnp.float32),
            pltpu.VMEM((ticks - 1, CHUNKS * rows, positions // CHUNKS), jnp.float32),
            pltpu.SemaphoreType.DMA((9,)),
            pltpu.SemaphoreType.DMA((slots, length, UNITS)),
            pltpu.SemaphoreType.DMA((slots, length, len(PARTS))),
            pltpu.SemaphoreType.DMA((slots,)),
            pltpu.SemaphoreType.DMA((slots, 2, length)),
            pltpu.SemaphoreType.DMA((slots, length)),
            pltpu.SemaphoreType.DMA((ticks - 1, 3)),
        ],
        compiler_params=pltpu.CompilerParams(
            collective_id=0, has_side_effects=True, vmem_limit_bytes=63 * 1024 * 1024
        ),
    )(resident[0], held_skip[0], fresh, first_weight, second_weight)
    return out[None]


def solution(mesh):
    return jax.shard_map(
        functools.partial(body, mesh.shape["segment"], mesh.shape["chan"]),
        mesh=mesh,
        in_specs=(
            P("segment", "chan", None),
            P("segment", "chan", None),
            P(None, "chan", None),
            P("segment", "chan", None),
            P("segment", "chan", None),
        ),
        out_specs=P("segment", "chan", None),
        check_vma=False,
    )
```

```python
import functools

import jax
import jax.numpy as jnp
from jax import lax
from jax.experimental import pallas as pl
from jax.experimental.pallas import tpu as pltpu
from jax.sharding import PartitionSpec as P

ROWS = 16
COLS = 32
MESH = pl.DeviceIdType.MESH
HALVES = 2
PIECES = 2
CHUNKS = HALVES * PIECES
UNITS = 8
OWN_UNITS = 5
CUTS = sorted({0, UNITS // 2, OWN_UNITS, UNITS})
PARTS = tuple(zip(CUTS[:-1], CUTS[1:]))


def silu(v):
    return v / (1.0 + jnp.exp(-v))


def block_of(rows):
    for size in (32, 40, 16):
        if rows % size == 0:
            return size
    return 8


def first_decoder_tick(segments, ticks):
    return max(0, ticks - segments // 2)


def kernel(
    segments, n, ticks,
    resident, held_skip, fresh, first_weight, second_weight, out_ref,
    stage, wv, g, operand, acc, passed_out,
    w_sem, recv_sem, swap_sem, partner_sem, z_sem, y_sem, pass_sem,
):
    seg = lax.axis_index("segment")
    me = lax.axis_index("chan")
    place = me // 2
    core = me % 2
    partner = me + 1 - 2 * core
    length = n // 2
    half = segments // 2
    encoder = seg < half
    decoder = jnp.logical_not(encoder)
    first_tick = first_decoder_tick(segments, ticks)
    merge = first_tick >= 1
    merged = (seg == half) & merge
    rows, positions = resident.shape
    part_positions = positions // HALVES
    piece = positions // CHUNKS
    width = 2 * rows
    channels = length * width
    blk = block_of(rows)
    split_blk = 32 if rows % 32 == 0 else rows
    twin = jnp.where(encoder, seg + half, seg - half)

    def load(conv, tap, slot):
        source = (first_weight, second_weight)[conv]
        columns = pl.ds(pl.multiple_of(tap * channels, 128), channels)
        return pltpu.make_async_copy(source.at[0, :, columns], stage.at[slot], w_sem.at[slot])

    def store_split(conv, tap, value_of):
        def some_rows(i, _):
            start = i * split_blk
            if split_blk != rows:
                start = pl.multiple_of(start, 16)
            spot = pl.ds(pl.multiple_of(tap * rows + start, 16), split_blk)
            for q in range(length):
                value = value_of(pl.ds(start, split_blk), slice(q * width, (q + 1) * width))
                high = value.astype(jnp.bfloat16)
                low = (value - high.astype(jnp.float32)).astype(jnp.bfloat16)
                wv[conv, q, spot, 0:width] = high
                wv[conv, q, spot, width : 2 * width] = low
                wv[conv, q, spot, 2 * width : 3 * width] = high
            return 0
        lax.fori_loop(0, rows // split_blk, some_rows, 0)

    depth = 4

    def start_first_loads():
        @pl.when(jnp.logical_not(merged))
        def _():
            def one(tap, _):
                load(0, tap, tap).start()
                return 0
            lax.fori_loop(0, 9, one, 0)

        if merge:
            @pl.when(merged)
            def _():
                for tap in range(depth):
                    load(0, tap, tap).start()
                    load(1, tap, depth + tap).start()

    def split_taps(conv, low, high):
        def one(tap, _):
            load(0, 0, tap).wait()
            store_split(conv, tap, lambda r, c: stage[tap, r, c])
            return 0
        lax.fori_loop(low, high, one, 0)

    def reload_taps(low, high):
        def one(tap, _):
            load(1, tap, tap).start()
            return 0
        lax.fori_loop(low, high, one, 0)

    def split_merged(low, high):
        def one(tap, _):
            a = tap % depth
            load(0, 0, a).wait()
            load(1, 0, depth + a).wait()
            store_split(0, tap, lambda r, c: stage[a, r, c] + stage[depth + a, r, c])

            @pl.when(tap + depth < 9)
            def _():
                load(0, tap + depth, a).start()
                load(1, tap + depth, depth + a).start()
            return 0
        lax.fori_loop(low, high, one, 0)

    start_first_loads()

    barrier = pltpu.get_barrier_semaphore()

    def greet(cond, segment, chan):
        @pl.when(cond)
        def _():
            pl.semaphore_signal(barrier, inc=1, device_id=(segment, chan), device_id_type=MESH)
        return jnp.where(cond, 1, 0)

    def kept(s):
        return jnp.clip(s, 0, segments - 1)

    greeted = greet(seg >= 0, seg, partner)
    for p in range(length):
        greeted += greet(place != p, seg, 2 * p + core)
        greeted += greet(seg >= 0, twin, 2 * p + core)
    greeted += greet(seg > 0, kept(seg - 1), me)
    greeted += greet(seg < segments - 1, kept(seg + 1), me)
    greeted += greet(seg >= 0, segments - 1 - seg, me)
    greeted += greet(seg + 1 < half, kept(seg + 1 + half), me)
    greeted += greet(seg >= half + 1, kept(seg - 1 - half), me)

    def encoder_slot(t, kind):
        return 2 * t + kind

    def decoder_slot(t, kind):
        return 2 * ticks + 2 * jnp.maximum(t - first_tick, 0) + kind

    def decoder_active(s, t):
        return s + (ticks - 1 - t) <= segments - 1

    shared = (segments + half) // 2
    shares = seg == shared
    if (segments + half) % 2:
        shares = seg < 0

    unit = CHUNKS * rows // UNITS

    def units_of(u, count):
        return pl.ds(u * unit, count * unit)

    def copy(k, q, u, count, sem, target_seg, target):
        return pltpu.make_async_remote_copy(
            src_ref=g.at[k, core, q, units_of(u, count)],
            dst_ref=g.at[k, core, q, units_of(u, count)],
            send_sem=sem,
            recv_sem=recv_sem.at[k, q, u],
            device_id=(target_seg, target),
            device_id_type=MESH,
        )

    def swap(k, parity, q, part):
        low, high = PARTS[part]
        return pltpu.make_async_remote_copy(
            src_ref=g.at[k, parity, q, units_of(low, high - low)],
            dst_ref=g.at[k, parity, q, units_of(low, high - low)],
            send_sem=partner_sem.at[k],
            recv_sem=swap_sem.at[k, q, part],
            device_id=(seg, partner),
            device_id_type=MESH,
        )

    def across(k, q, u):
        return copy(k, q, u, 1, y_sem.at[k, q], twin, me)

    def arrived(k, q, u):
        copy(k, q, u, 1, y_sem.at[k, q], twin, me).wait_recv()

    near = jnp.minimum(place, length - 1 - place)
    at_end = near == 0
    inner = jnp.where(place < length // 2, 1, -1)

    def along(k, q, u, lane, target, relay):
        target = jnp.clip(target, 0, length - 1)
        ending = (target == 0) | (target == length - 1)
        to = jnp.where(relay & (at_end | ending), twin, seg)
        return copy(k, q, u, 1, z_sem.at[k, lane, q], to, 2 * target + core)

    def send_near(k, u, relay):
        along(k, place, u, 0, place + inner, relay).start()

        @pl.when(jnp.logical_not(at_end))
        def _():
            along(k, place, u, 1, place - inner, relay).start()

    def send_far(k):
        @pl.when(at_end)
        def _():
            for d in range(2, length):
                for u in range(OWN_UNITS, UNITS):
                    along(k, place, u, 1, place + inner * d, True).start()

    def twin_holds(q):
        return (q > 0) & (q < length - 1) & jnp.logical_not(at_end)

    def onward(k, q, u, relay):
        @pl.when(twin_holds(q) if relay else jnp.logical_not(at_end))
        def _():
            along(k, q, u, 0, place + jnp.where(q < place, 1, -1), relay).start()

    def swap_after(k, q, u):
        for part, (low, high) in enumerate(PARTS):
            if u == high - 1:
                swap(k, core, q, part).start()

    def source_of(i):
        paired = i < 2 * near
        d = jnp.where(paired, i // 2 + 1, i - near + 1)
        way = jnp.where(paired & (i % 2 == 1), -inner, inner)
        return place + way * d

    def multiply(k, w, q, h):
        for i in range(2):
            for p in range(PIECES):
                part = g[k, i, q, pl.ds((PIECES * h + p) * rows, rows)]
                high = part.astype(jnp.bfloat16)
                low = (part - high.astype(jnp.float32)).astype(jnp.bfloat16)
                cut = slice(p * piece, (p + 1) * piece)
                operand[i * rows : (i + 1) * rows, cut] = high
                operand[width + i * rows : width + (i + 1) * rows, cut] = high
                operand[2 * width + i * rows : 2 * width + (i + 1) * rows, cut] = low
        acc[h] += jnp.dot(wv[w, q], operand[...], preferred_element_type=jnp.float32)

    spot = lax.broadcasted_iota(jnp.int32, (blk, positions), 1)
    column = spot % COLS

    def placed(start):
        total = None
        for dx in (-1, 0, 1):
            column_sum = None
            for dy in (-1, 0, 1):
                tap = 3 * (dy + 1) + dx + 1
                at = pl.ds(pl.multiple_of(tap * rows + start, 8), blk)
                part = jnp.concatenate([acc[h, at, :] for h in range(HALVES)], axis=1)
                if dy:
                    part = pltpu.roll(part, (-dy * COLS) % positions, 1)
                    source = spot + dy * COLS
                    part = jnp.where((source >= 0) & (source < positions), part, 0.0)
                column_sum = part if column_sum is None else column_sum + part
            if dx:
                column_sum = pltpu.roll(column_sum, (-dx) % positions, 1)
                source = column + dx
                column_sum = jnp.where((source >= 0) & (source < COLS), column_sum, 0.0)
            total = column_sum if total is None else total + column_sum
        return total

    def over_rows(action):
        def one(i, _):
            start = pl.multiple_of(i * blk, 8)
            action(start, pl.ds(start, blk))
            return 0
        lax.fori_loop(0, rows // blk, one, 0)

    def cut_of(c):
        return slice(c * piece, (c + 1) * piece)

    def rows_at(c, start=0, count=None):
        return pl.ds(c * rows + start, rows if count is None else count)

    def fill(k, source):
        for c in range(CHUNKS):
            g[k, core, place, rows_at(c)] = source[:, cut_of(c)]

    @pl.when(encoder)
    def _():
        fill(0, resident)

    if first_tick == 0:
        @pl.when(decoder)
        def _():
            fill(2 * ticks, resident)
            fill(2 * ticks + 1, held_skip)

    @pl.when((seg == 0) | (seg == half))
    def _():
        for t in range(1, ticks):
            fill(2 * t, fresh.at[t - 1])

    pl.semaphore_wait(barrier, greeted)

    def drain_along(k, low, high, relay):
        def sent(q, lane):
            copy(k, q, low, high - low, z_sem.at[k, lane, q], seg, partner).wait_send()

        sent(place, 0)

        @pl.when(at_end & relay)
        def _():
            if length > 2:
                span = g.at[k, core, pl.ds(0, length - 2), units_of(low, high - low)]
                pltpu.make_async_remote_copy(
                    src_ref=span, dst_ref=span,
                    send_sem=z_sem.at[k, 1, place], recv_sem=recv_sem.at[k, 0, 0],
                    device_id=(seg, partner), device_id_type=MESH,
                ).wait_send()

        @pl.when(jnp.logical_not(at_end))
        def _():
            sent(place, 1)

            def one(q, _):
                @pl.when(q != place)
                def _():
                    sent(q, 0)
                return 0
            lax.fori_loop(int(relay), length - int(relay), one, 0)

    def drain_partner(k):
        pltpu.make_async_remote_copy(
            src_ref=g.at[k, core], dst_ref=g.at[k, core],
            send_sem=partner_sem.at[k], recv_sem=swap_sem.at[k, 0, 0],
            device_id=(seg, partner), device_id_type=MESH,
        ).wait_send()

    def drain_across(k, q, low, high):
        copy(k, q, low, high - low, y_sem.at[k, q], twin, me).wait_send()

    twin_of = jnp.where(encoder, seg, twin)

    def facts_of(idx):
        t = idx // 2
        kind = idx % 2
        skip_held = shares & (kind == 1) & (t > 0)
        k = jnp.where(
            encoder,
            encoder_slot(t, kind),
            jnp.where(skip_held, encoder_slot(t, 0), decoder_slot(t, kind)),
        )
        active = encoder | (decoder_active(seg, t) & jnp.logical_not(merged & (kind == 1)))
        solo = (twin_of == 0) & (idx == 2 * ticks - 1)
        lifts = encoder & ((kind == 1) | (t == 0)) & jnp.logical_not(solo)
        lends = encoder & (twin == shared) & (kind == 0) & (t > 0) & decoder_active(twin, t)
        if (segments + half) % 2:
            lends = lends & (seg < 0)
        return t, kind, k, active, lifts, lends, solo, skip_held

    def drain(idx):
        t, kind, k, active, lifts, lends, solo, skip_held = facts_of(idx)
        relayed = encoder_slot(t, kind)

        @pl.when(active)
        def _():
            drain_partner(k)

            @pl.when(encoder & jnp.logical_not(solo))
            def _():
                drain_along(k, 0, OWN_UNITS, False)

                @pl.when(lifts)
                def _():
                    drain_across(k, place, OWN_UNITS, UNITS)

                @pl.when(lends)
                def _():
                    def one(q, _):
                        partly = (q == place) | twin_holds(q)

                        @pl.when(partly)
                        def _():
                            drain_across(k, q, 0, OWN_UNITS)

                        @pl.when(jnp.logical_not(partly))
                        def _():
                            drain_across(k, q, 0, UNITS)
                        return 0
                    lax.fori_loop(0, length, one, 0)

            @pl.when((decoder & jnp.logical_not(skip_held)) | (encoder & solo))
            def _():
                drain_along(k, 0, UNITS, False)

        @pl.when(decoder & jnp.logical_not(solo))
        def _():
            drain_along(relayed, OWN_UNITS, UNITS, True)

            @pl.when((seg != half) & (kind == 0) & (t > 0))
            def _():
                drain_across(relayed, place, OWN_UNITS, UNITS)

            @pl.when(jnp.logical_not(at_end))
            def _():
                def one(q, _):
                    @pl.when(q != place)
                    def _():
                        drain_across(relayed, q, OWN_UNITS, UNITS)
                    return 0
                lax.fori_loop(1, length - 1, one, 0)

    others = length - 1
    slots = 2 * length
    third = slots - 4

    def event_of(e):
        h = e // others
        m = (e + 1) // 2
        eh = jnp.where(e == 0, 0, jnp.where(e == 2 * others - 1, 1, (e + 1) % 2))
        ei = jnp.where(e == 0, 0, jnp.where(e % 2 == 1, jnp.minimum(m, others - 1), e // 2 - 1))
        return jnp.where(at_end, ei, e - h * others), jnp.where(at_end, eh, h)

    def went_early(idx):
        facts = facts_of(idx)
        return (seg == half) & facts[3] & jnp.logical_not(facts[-1])

    def relay_own(idx):
        t = idx // 2
        kind = idx % 2
        relayed = encoder_slot(t, kind)
        handed = (kind == 0) & (t > 0)
        for u in range(OWN_UNITS, UNITS):
            @pl.when(jnp.logical_not((seg == half) & handed))
            def _():
                arrived(relayed, place, u)

            @pl.when((seg != half) & handed)
            def _():
                across(relayed, place, u).start()
            send_near(relayed, u, True)
        send_far(relayed)

    def relay_others(idx):
        relayed = encoder_slot(idx // 2, idx % 2)

        def one(i, _):
            q = source_of(i)

            @pl.when(twin_holds(q))
            def _():
                for u in range(OWN_UNITS, UNITS):
                    arrived(relayed, q, u)
                    onward(relayed, q, u, True)
                    across(relayed, q, u).start()
            return 0
        lax.fori_loop(0, others, one, 0)

    def one_stage(idx, _):
        t, kind, k, active, lifts, lends, solo, skip_held = facts_of(idx)
        local = jnp.where(encoder, (kind == 1) | (t == 0) | (seg == 0), t == 0)
        ahead = encoder & (kind == 0) & (t > 0) & ((seg == 0) | (t > 1))

        @pl.when(decoder & jnp.logical_not(solo | ((idx > 0) & went_early(idx - 1))))
        def _():
            relay_own(idx)
            relay_others(idx)

        @pl.when(active)
        def _():
            for u in range(OWN_UNITS):
                @pl.when(jnp.logical_not(local | ahead))
                def _():
                    arrived(k, place, u)

                @pl.when(jnp.logical_not(ahead | skip_held))
                def _():
                    send_near(k, u, False)

                @pl.when(lends)
                def _():
                    across(k, place, u).start()
                swap_after(k, place, u)

            @pl.when(local | decoder)
            def _():
                for u in range(OWN_UNITS, UNITS):
                    @pl.when(jnp.logical_not(local | skip_held))
                    def _():
                        arrived(k, place, u)

                    @pl.when((decoder & jnp.logical_not(skip_held)) | (encoder & solo))
                    def _():
                        send_near(k, u, False)

                    @pl.when(lifts)
                    def _():
                        across(k, place, u).start()
                    swap_after(k, place, u)

            @pl.when(encoder & (kind == 1) & facts_of(jnp.maximum(idx - 1, 0))[5])
            def _():
                q = source_of(others - 1)
                for u in range(UNITS):
                    if u < OWN_UNITS:
                        across(k - 1, q, u).start()
                    else:
                        @pl.when(jnp.logical_not(twin_holds(q)))
                        def _():
                            across(k - 1, q, u).start()

            @pl.when(encoder | (kind == 0))
            def _():
                acc[...] = jnp.zeros_like(acc)

        @pl.when(idx > 1)
        def _():
            drain(idx - 2)

        @pl.when(encoder & (idx == 0))
        def _():
            split_taps(0, 0, 9)
            reload_taps(0, 9)

        def one_slot(s, _):
            @pl.when((idx < 2 * ticks - 2) & went_early(idx))
            def _():
                @pl.when(s == 3)
                def _():
                    relay_own(idx + 1)

                @pl.when(s == 4)
                def _():
                    relay_others(idx + 1)

            e, part = event_of(jnp.maximum(s - 1, 0))
            gathers = active & (s >= 1) & (s <= 2 * others)

            @pl.when(gathers & (part == 0))
            def _():
                q = source_of(e)
                for u in range(OWN_UNITS):
                    arrived(k, q, u)

                    @pl.when(jnp.logical_not(skip_held))
                    def _():
                        onward(k, q, u, False)

                    @pl.when(lends & (e < others - 1))
                    def _():
                        across(k, q, u).start()
                    swap_after(k, q, u)

            @pl.when(gathers & (part == 1))
            def _():
                q = source_of(e)
                for u in range(OWN_UNITS, UNITS):
                    @pl.when(jnp.logical_not(skip_held & twin_holds(q)))
                    def _():
                        arrived(k, q, u)

                    @pl.when(lends & (e < others - 1) & jnp.logical_not(twin_holds(q)))
                    def _():
                        across(k, q, u).start()

                    @pl.when((decoder & jnp.logical_not(skip_held)) | (encoder & solo))
                    def _():
                        onward(k, q, u, False)
                    swap_after(k, q, u)

            @pl.when(
                encoder & (kind == 1) & (t < ticks - 1) & ((seg == 0) | (t > 0))
                & (s == jnp.where(seg == 0, 2 * others - 1, slots - 1))
            )
            def _():
                for u in range(OWN_UNITS):
                    @pl.when(seg > 0)
                    def _():
                        arrived(k + 1, place, u)
                    send_near(k + 1, u, False)

            @pl.when(encoder & jnp.logical_not(local) & (s == 1))
            def _():
                for u in range(OWN_UNITS, UNITS):
                    arrived(k, place, u)
                    swap_after(k, place, u)

            @pl.when(encoder & (idx == 0) & (s >= 1) & (s < 4))
            def _():
                split_taps(1, 3 * s - 3, 3 * s)

            @pl.when((s >= third) & (s < third + 3))
            def _():
                low = 3 * (s - third)

                @pl.when(decoder & jnp.logical_not(merged) & (idx == 0))
                def _():
                    split_taps(0, low, low + 3)
                    reload_taps(low, low + 3)

                @pl.when(decoder & jnp.logical_not(merged) & (idx == 1))
                def _():
                    split_taps(1, low, low + 3)

                if merge:
                    @pl.when(merged & (idx == 0))
                    def _():
                        split_merged(low, low + 3)

            @pl.when(active)
            def _():
                i, h = event_of(jnp.maximum(s - 2, 0))
                q = jnp.where(s < 2, place, source_of(i))
                h = jnp.where(s < 2, s, h)

                for side in range(HALVES):
                    @pl.when(h == side)
                    def _():
                        for part, (low, _) in enumerate(PARTS):
                            if low // (UNITS // HALVES) == side:
                                swap(k, 1 - core, q, part).wait_recv()
                multiply(k, kind, q, h)
            return 0
        lax.fori_loop(0, slots, one_slot, 0)

        def after(start, rows_of):
            value = placed(start)

            def put(parts):
                @pl.when(t == ticks - 1)
                def _():
                    for c in range(CHUNKS):
                        out_ref[rows_of, cut_of(c)] = parts[c]

                @pl.when(t < ticks - 1)
                def _():
                    for c in range(CHUNKS):
                        passed_out[jnp.minimum(t, ticks - 2), rows_at(c, start, blk), :] = parts[c]

            @pl.when(encoder & (kind == 0))
            def _():
                result = silu(value)
                for c in range(CHUNKS):
                    g[k + 1, core, place, rows_at(c, start, blk), :] = result[:, cut_of(c)]

            @pl.when(encoder & (kind == 1))
            def _():
                put([
                    g[k - 1, core, place, rows_at(c, start, blk), :] + value[:, cut_of(c)]
                    for c in range(CHUNKS)
                ])

            @pl.when(decoder)
            def _():
                result = silu(value)
                put([result[:, cut_of(c)] for c in range(CHUNKS)])

        ends = active & ((kind == 1) | merged)

        @pl.when(encoder | ends)
        def _():
            over_rows(after)

        @pl.when(ends & (t < ticks - 1))
        def _():
            give_all(t, True)
        return 0

    def give(t, kind, u, count):
        into_encoder = seg + 1 < half
        slot = (
            jnp.where(into_encoder, encoder_slot(t + 1, 0), decoder_slot(t + 1, 0)),
            encoder_slot(t + 1, 0),
            decoder_slot(t + 1, 1),
        )[kind]
        target = (kept(seg + 1), kept(seg + 1 + half), segments - 1 - seg)[kind]
        return pltpu.make_async_remote_copy(
            src_ref=passed_out.at[t, units_of(u, count)],
            dst_ref=g.at[slot, core, place, units_of(u, count)],
            send_sem=pass_sem.at[t, kind],
            recv_sem=recv_sem.at[slot, place, u],
            device_id=(target, me),
            device_id_type=MESH,
        )

    def give_all(t, starting):
        next_in = (seg + 1 < half) | ((seg < segments - 1) & decoder_active(seg + 1, t + 1))
        helper = seg + 1 < half
        mirror = segments - 1 - seg
        skip = encoder & decoder_active(mirror, t + 1)
        if merge:
            skip = skip & (mirror != half)
        if (segments + half) % 2 == 0:
            skip = skip & (mirror != shared)
        mixed = sorted(range(UNITS), key=lambda u: (u % OWN_UNITS, u))
        if starting:
            @pl.when(helper)
            def _():
                for u in mixed:
                    give(t, 0 if u < OWN_UNITS else 1, u, 1).start()

            @pl.when(next_in & jnp.logical_not(helper))
            def _():
                for u in range(UNITS):
                    give(t, 0, u, 1).start()

            @pl.when(skip)
            def _():
                for u in range(UNITS):
                    give(t, 2, u, 1).start()
        else:
            @pl.when(helper)
            def _():
                give(t, 0, 0, OWN_UNITS).wait_send()
                give(t, 1, OWN_UNITS, UNITS - OWN_UNITS).wait_send()

            @pl.when(next_in & jnp.logical_not(helper))
            def _():
                give(t, 0, 0, UNITS).wait_send()

            @pl.when(skip)
            def _():
                give(t, 2, 0, UNITS).wait_send()

    lax.fori_loop(0, 2 * ticks, one_stage, 0)
    for idx in range(max(0, 2 * ticks - 2), 2 * ticks):
        drain(idx)

    for t in range(ticks - 1):
        @pl.when(encoder | decoder_active(seg, t))
        def _():
            give_all(t, False)


def body(segments, n, resident, held_skip, fresh, first_weight, second_weight):
    ticks = fresh.shape[0] + 1
    rows, positions = resident.shape[1:]
    length = n // 2
    width = 2 * rows
    slots = 2 * ticks + 2 * (ticks - first_decoder_tick(segments, ticks))
    vmem = pl.BlockSpec(memory_space=pltpu.VMEM)
    anywhere = pl.BlockSpec(memory_space=pl.ANY)
    out = pl.pallas_call(
        functools.partial(kernel, segments, n, ticks),
        out_shape=jax.ShapeDtypeStruct((rows, positions), jnp.float32),
        in_specs=[vmem, vmem, vmem, anywhere, anywhere],
        out_specs=vmem,
        scratch_shapes=[
            pltpu.VMEM((9, rows, length * width), jnp.float32),
            pltpu.VMEM((2, length, 9 * rows, 3 * width), jnp.bfloat16),
            pltpu.VMEM((slots, 2, length, CHUNKS * rows, positions // CHUNKS), jnp.float32),
            pltpu.VMEM((3 * width, positions // HALVES), jnp.bfloat16),
            pltpu.VMEM((HALVES, 9 * rows, positions // HALVES), jnp.float32),
            pltpu.VMEM((ticks - 1, CHUNKS * rows, positions // CHUNKS), jnp.float32),
            pltpu.SemaphoreType.DMA((9,)),
            pltpu.SemaphoreType.DMA((slots, length, UNITS)),
            pltpu.SemaphoreType.DMA((slots, length, len(PARTS))),
            pltpu.SemaphoreType.DMA((slots,)),
            pltpu.SemaphoreType.DMA((slots, 2, length)),
            pltpu.SemaphoreType.DMA((slots, length)),
            pltpu.SemaphoreType.DMA((ticks - 1, 3)),
        ],
        compiler_params=pltpu.CompilerParams(
            collective_id=0, has_side_effects=True, vmem_limit_bytes=63 * 1024 * 1024
        ),
    )(resident[0], held_skip[0], fresh, first_weight, second_weight)
    return out[None]


def solution(mesh):
    return jax.shard_map(
        functools.partial(body, mesh.shape["segment"], mesh.shape["chan"]),
        mesh=mesh,
        in_specs=(
            P("segment", "chan", None),
            P("segment", "chan", None),
            P(None, "chan", None),
            P("segment", "chan", None),
            P("segment", "chan", None),
        ),
        out_specs=P("segment", "chan", None),
        check_vma=False,
    )
```

```python
import functools

import jax
import jax.numpy as jnp
from jax import lax
from jax.experimental import pallas as pl
from jax.experimental.pallas import tpu as pltpu
from jax.sharding import PartitionSpec as P

ROWS = 16
COLS = 32
MESH = pl.DeviceIdType.MESH
HALVES = 2
PIECES = 2
CHUNKS = HALVES * PIECES
UNITS = 8
OWN_UNITS = 5
CUTS = sorted({0, UNITS // 2, OWN_UNITS, UNITS})
PARTS = tuple(zip(CUTS[:-1], CUTS[1:]))


def silu(v):
    return v / (1.0 + jnp.exp(-v))


def first_decoder_tick(segments, ticks):
    return max(0, ticks - segments // 2)


def kernel(
    segments, n, ticks,
    resident, held_skip, fresh, first_weight, second_weight, out_ref,
    stage, wv, g, operand, acc, passed_out,
    w_sem, recv_sem, swap_sem, partner_sem, z_sem, y_sem, pass_sem,
):
    seg = lax.axis_index("segment")
    me = lax.axis_index("chan")
    place = me // 2
    core = me % 2
    partner = me + 1 - 2 * core
    length = n // 2
    half = segments // 2
    encoder = seg < half
    decoder = jnp.logical_not(encoder)
    first_tick = first_decoder_tick(segments, ticks)
    merge = first_tick >= 1
    merged = (seg == half) & merge
    rows, positions = resident.shape
    part_positions = positions // HALVES
    piece = positions // CHUNKS
    width = 2 * rows
    channels = length * width
    blk = rows
    twin = jnp.where(encoder, seg + half, seg - half)

    def load(conv, tap, slot):
        source = (first_weight, second_weight)[conv]
        columns = pl.ds(pl.multiple_of(tap * channels, 128), channels)
        return pltpu.make_async_copy(source.at[0, :, columns], stage.at[slot], w_sem.at[slot])

    def store_split(conv, tap, value_of):
        spot = pl.ds(pl.multiple_of(tap * rows, 16 if rows % 16 == 0 else 8), rows)
        for q in range(length):
            value = value_of(slice(q * width, (q + 1) * width))
            high = value.astype(jnp.bfloat16)
            low = (value - high.astype(jnp.float32)).astype(jnp.bfloat16)
            wv[conv, q, spot, 0:width] = high
            wv[conv, q, spot, width : 2 * width] = low
            wv[conv, q, spot, 2 * width : 3 * width] = high

    depth = 4

    def start_first_loads():
        @pl.when(jnp.logical_not(merged))
        def _():
            def one(tap, _):
                load(0, tap, tap).start()
                return 0
            lax.fori_loop(0, 9, one, 0)

        if merge:
            @pl.when(merged)
            def _():
                for tap in range(depth):
                    load(0, tap, tap).start()
                    load(1, tap, depth + tap).start()

    def split_taps(conv, low, high):
        def one(tap, _):
            load(0, 0, tap).wait()
            store_split(conv, tap, lambda c: stage[tap, :, c])
            return 0
        lax.fori_loop(low, high, one, 0)

    def reload_taps(low, high):
        def one(tap, _):
            load(1, tap, tap).start()
            return 0
        lax.fori_loop(low, high, one, 0)

    def split_merged(low, high):
        def one(tap, _):
            a = tap % depth
            load(0, 0, a).wait()
            load(1, 0, depth + a).wait()
            store_split(0, tap, lambda c: stage[a, :, c] + stage[depth + a, :, c])

            @pl.when(tap + depth < 9)
            def _():
                load(0, tap + depth, a).start()
                load(1, tap + depth, depth + a).start()
            return 0
        lax.fori_loop(low, high, one, 0)

    start_first_loads()

    barrier = pltpu.get_barrier_semaphore()

    def greet(cond, segment, chan):
        @pl.when(cond)
        def _():
            pl.semaphore_signal(barrier, inc=1, device_id=(segment, chan), device_id_type=MESH)
        return jnp.where(cond, 1, 0)

    def kept(s):
        return jnp.clip(s, 0, segments - 1)

    greeted = greet(seg >= 0, seg, partner)
    for p in range(length):
        greeted += greet(place != p, seg, 2 * p + core)
        greeted += greet(seg >= 0, twin, 2 * p + core)
    greeted += greet(seg > 0, kept(seg - 1), me)
    greeted += greet(seg < segments - 1, kept(seg + 1), me)
    greeted += greet(seg >= 0, segments - 1 - seg, me)
    greeted += greet(seg + 1 < half, kept(seg + 1 + half), me)
    greeted += greet(seg >= half + 1, kept(seg - 1 - half), me)

    def encoder_slot(t, kind):
        return 2 * t + kind

    def decoder_slot(t, kind):
        return 2 * ticks + 2 * jnp.maximum(t - first_tick, 0) + kind

    def decoder_active(s, t):
        return s + (ticks - 1 - t) <= segments - 1

    shared = (segments + half) // 2
    shares = seg == shared
    if (segments + half) % 2:
        shares = seg < 0

    unit = CHUNKS * rows // UNITS

    def units_of(u, count):
        return pl.ds(u * unit, count * unit)

    def copy(k, q, u, count, sem, target_seg, target):
        return pltpu.make_async_remote_copy(
            src_ref=g.at[k, core, q, units_of(u, count)],
            dst_ref=g.at[k, core, q, units_of(u, count)],
            send_sem=sem,
            recv_sem=recv_sem.at[k, q, u],
            device_id=(target_seg, target),
            device_id_type=MESH,
        )

    def swap(k, parity, q, part):
        low, high = PARTS[part]
        return pltpu.make_async_remote_copy(
            src_ref=g.at[k, parity, q, units_of(low, high - low)],
            dst_ref=g.at[k, parity, q, units_of(low, high - low)],
            send_sem=partner_sem.at[k],
            recv_sem=swap_sem.at[k, q, part],
            device_id=(seg, partner),
            device_id_type=MESH,
        )

    def across(k, q, u):
        return copy(k, q, u, 1, y_sem.at[k, q], twin, me)

    def arrived(k, q, u):
        copy(k, q, u, 1, y_sem.at[k, q], twin, me).wait_recv()

    near = jnp.minimum(place, length - 1 - place)
    at_end = near == 0
    inner = jnp.where(place < length // 2, 1, -1)

    def along(k, q, u, lane, target, relay):
        target = jnp.clip(target, 0, length - 1)
        ending = (target == 0) | (target == length - 1)
        to = jnp.where(relay & (at_end | ending), twin, seg)
        return copy(k, q, u, 1, z_sem.at[k, lane, q], to, 2 * target + core)

    def send_near(k, u, relay):
        along(k, place, u, 0, place + inner, relay).start()

        @pl.when(jnp.logical_not(at_end))
        def _():
            along(k, place, u, 1, place - inner, relay).start()

    def send_far(k):
        @pl.when(at_end)
        def _():
            for d in range(2, length):
                for u in range(OWN_UNITS, UNITS):
                    along(k, place, u, 1, place + inner * d, True).start()

    def twin_holds(q):
        return (q > 0) & (q < length - 1) & jnp.logical_not(at_end)

    def onward(k, q, u, relay):
        @pl.when(twin_holds(q) if relay else jnp.logical_not(at_end))
        def _():
            along(k, q, u, 0, place + jnp.where(q < place, 1, -1), relay).start()

    def swap_after(k, q, u):
        for part, (low, high) in enumerate(PARTS):
            if u == high - 1:
                swap(k, core, q, part).start()

    def source_of(i):
        paired = i < 2 * near
        d = jnp.where(paired, i // 2 + 1, i - near + 1)
        way = jnp.where(paired & (i % 2 == 1), -inner, inner)
        return place + way * d

    def multiply(k, w, q, h):
        for i in range(2):
            for p in range(PIECES):
                part = g[k, i, q, pl.ds((PIECES * h + p) * rows, rows)]
                high = part.astype(jnp.bfloat16)
                low = (part - high.astype(jnp.float32)).astype(jnp.bfloat16)
                cut = slice(p * piece, (p + 1) * piece)
                operand[i * rows : (i + 1) * rows, cut] = high
                operand[width + i * rows : width + (i + 1) * rows, cut] = high
                operand[2 * width + i * rows : 2 * width + (i + 1) * rows, cut] = low
        acc[h] += jnp.dot(wv[w, q], operand[...], preferred_element_type=jnp.float32)

    spot = lax.broadcasted_iota(jnp.int32, (blk, positions), 1)
    column = spot % COLS

    def placed(start):
        total = None
        for dx in (-1, 0, 1):
            column_sum = None
            for dy in (-1, 0, 1):
                tap = 3 * (dy + 1) + dx + 1
                at = pl.ds(pl.multiple_of(tap * rows + start, 8), blk)
                part = jnp.concatenate([acc[h, at, :] for h in range(HALVES)], axis=1)
                if dy:
                    part = pltpu.roll(part, (-dy * COLS) % positions, 1)
                    source = spot + dy * COLS
                    part = jnp.where((source >= 0) & (source < positions), part, 0.0)
                column_sum = part if column_sum is None else column_sum + part
            if dx:
                column_sum = pltpu.roll(column_sum, (-dx) % positions, 1)
                source = column + dx
                column_sum = jnp.where((source >= 0) & (source < COLS), column_sum, 0.0)
            total = column_sum if total is None else total + column_sum
        return total

    def over_rows(action):
        def one(i, _):
            start = pl.multiple_of(i * blk, 8)
            action(start, pl.ds(start, blk))
            return 0
        lax.fori_loop(0, rows // blk, one, 0)

    def cut_of(c):
        return slice(c * piece, (c + 1) * piece)

    def rows_at(c, start=0, count=None):
        return pl.ds(c * rows + start, rows if count is None else count)

    def fill(k, source):
        for c in range(CHUNKS):
            g[k, core, place, rows_at(c)] = source[:, cut_of(c)]

    @pl.when(encoder)
    def _():
        fill(0, resident)

    if first_tick == 0:
        @pl.when(decoder)
        def _():
            fill(2 * ticks, resident)
            fill(2 * ticks + 1, held_skip)

    @pl.when((seg == 0) | (seg == half))
    def _():
        for t in range(1, ticks):
            fill(2 * t, fresh.at[t - 1])

    pl.semaphore_wait(barrier, greeted)

    def drain_along(k, low, high, relay):
        def sent(q, lane):
            copy(k, q, low, high - low, z_sem.at[k, lane, q], seg, partner).wait_send()

        sent(place, 0)

        @pl.when(at_end & relay)
        def _():
            if length > 2:
                span = g.at[k, core, pl.ds(0, length - 2), units_of(low, high - low)]
                pltpu.make_async_remote_copy(
                    src_ref=span, dst_ref=span,
                    send_sem=z_sem.at[k, 1, place], recv_sem=recv_sem.at[k, 0, 0],
                    device_id=(seg, partner), device_id_type=MESH,
                ).wait_send()

        @pl.when(jnp.logical_not(at_end))
        def _():
            sent(place, 1)

            def one(q, _):
                @pl.when(q != place)
                def _():
                    sent(q, 0)
                return 0
            lax.fori_loop(int(relay), length - int(relay), one, 0)

    def drain_partner(k):
        pltpu.make_async_remote_copy(
            src_ref=g.at[k, core], dst_ref=g.at[k, core],
            send_sem=partner_sem.at[k], recv_sem=swap_sem.at[k, 0, 0],
            device_id=(seg, partner), device_id_type=MESH,
        ).wait_send()

    def drain_across(k, q, low, high):
        copy(k, q, low, high - low, y_sem.at[k, q], twin, me).wait_send()

    twin_of = jnp.where(encoder, seg, twin)

    def facts_of(idx):
        t = idx // 2
        kind = idx % 2
        skip_held = shares & (kind == 1) & (t > 0)
        k = jnp.where(
            encoder,
            encoder_slot(t, kind),
            jnp.where(skip_held, encoder_slot(t, 0), decoder_slot(t, kind)),
        )
        active = encoder | (decoder_active(seg, t) & jnp.logical_not(merged & (kind == 1)))
        solo = (twin_of == 0) & (idx == 2 * ticks - 1)
        lifts = encoder & ((kind == 1) | (t == 0)) & jnp.logical_not(solo)
        lends = encoder & (twin == shared) & (kind == 0) & (t > 0) & decoder_active(twin, t)
        if (segments + half) % 2:
            lends = lends & (seg < 0)
        return t, kind, k, active, lifts, lends, solo, skip_held

    def drain(idx):
        t, kind, k, active, lifts, lends, solo, skip_held = facts_of(idx)
        relayed = encoder_slot(t, kind)

        @pl.when(active)
        def _():
            drain_partner(k)

            @pl.when(encoder & jnp.logical_not(solo))
            def _():
                drain_along(k, 0, OWN_UNITS, False)

                @pl.when(lifts)
                def _():
                    drain_across(k, place, OWN_UNITS, UNITS)

                @pl.when(lends)
                def _():
                    def one(q, _):
                        partly = (q == place) | twin_holds(q)

                        @pl.when(partly)
                        def _():
                            drain_across(k, q, 0, OWN_UNITS)

                        @pl.when(jnp.logical_not(partly))
                        def _():
                            drain_across(k, q, 0, UNITS)
                        return 0
                    lax.fori_loop(0, length, one, 0)

            @pl.when((decoder & jnp.logical_not(skip_held)) | (encoder & solo))
            def _():
                drain_along(k, 0, UNITS, False)

        @pl.when(decoder & jnp.logical_not(solo))
        def _():
            drain_along(relayed, OWN_UNITS, UNITS, True)

            @pl.when((seg != half) & (kind == 0) & (t > 0))
            def _():
                drain_across(relayed, place, OWN_UNITS, UNITS)

            @pl.when(jnp.logical_not(at_end))
            def _():
                def one(q, _):
                    @pl.when(q != place)
                    def _():
                        drain_across(relayed, q, OWN_UNITS, UNITS)
                    return 0
                lax.fori_loop(1, length - 1, one, 0)

    others = length - 1
    slots = 2 * length
    third = slots - 4

    def event_of(e):
        h = e // others
        m = (e + 1) // 2
        eh = jnp.where(e == 0, 0, jnp.where(e == 2 * others - 1, 1, (e + 1) % 2))
        ei = jnp.where(e == 0, 0, jnp.where(e % 2 == 1, jnp.minimum(m, others - 1), e // 2 - 1))
        return jnp.where(at_end, ei, e - h * others), jnp.where(at_end, eh, h)

    def went_early(idx):
        facts = facts_of(idx)
        return (seg == half) & facts[3] & jnp.logical_not(facts[-1])

    def relay_own(idx):
        t = idx // 2
        kind = idx % 2
        relayed = encoder_slot(t, kind)
        handed = (kind == 0) & (t > 0)
        for u in range(OWN_UNITS, UNITS):
            @pl.when(jnp.logical_not((seg == half) & handed))
            def _():
                arrived(relayed, place, u)

            @pl.when((seg != half) & handed)
            def _():
                across(relayed, place, u).start()
            send_near(relayed, u, True)
        send_far(relayed)

    def relay_others(idx):
        relayed = encoder_slot(idx // 2, idx % 2)

        def one(i, _):
            q = source_of(i)

            @pl.when(twin_holds(q))
            def _():
                for u in range(OWN_UNITS, UNITS):
                    arrived(relayed, q, u)
                    onward(relayed, q, u, True)
                    across(relayed, q, u).start()
            return 0
        lax.fori_loop(0, others, one, 0)

    def one_stage(idx, _):
        t, kind, k, active, lifts, lends, solo, skip_held = facts_of(idx)
        local = jnp.where(encoder, (kind == 1) | (t == 0) | (seg == 0), t == 0)
        ahead = encoder & (kind == 0) & (t > 0) & ((seg == 0) | (t > 1))

        @pl.when(decoder & jnp.logical_not(solo | ((idx > 0) & went_early(idx - 1))))
        def _():
            relay_own(idx)
            relay_others(idx)

        @pl.when(active)
        def _():
            for u in range(OWN_UNITS):
                @pl.when(jnp.logical_not(local | ahead))
                def _():
                    arrived(k, place, u)

                @pl.when(jnp.logical_not(ahead | skip_held))
                def _():
                    send_near(k, u, False)

                @pl.when(lends)
                def _():
                    across(k, place, u).start()
                swap_after(k, place, u)

            @pl.when(local | decoder)
            def _():
                for u in range(OWN_UNITS, UNITS):
                    @pl.when(jnp.logical_not(local | skip_held))
                    def _():
                        arrived(k, place, u)

                    @pl.when((decoder & jnp.logical_not(skip_held)) | (encoder & solo))
                    def _():
                        send_near(k, u, False)

                    @pl.when(lifts)
                    def _():
                        across(k, place, u).start()
                    swap_after(k, place, u)

            @pl.when(encoder & (kind == 1) & facts_of(jnp.maximum(idx - 1, 0))[5])
            def _():
                q = source_of(others - 1)
                for u in range(UNITS):
                    if u < OWN_UNITS:
                        across(k - 1, q, u).start()
                    else:
                        @pl.when(jnp.logical_not(twin_holds(q)))
                        def _():
                            across(k - 1, q, u).start()

            @pl.when(encoder | (kind == 0))
            def _():
                acc[...] = jnp.zeros_like(acc)

        @pl.when(idx > 1)
        def _():
            drain(idx - 2)

        @pl.when(encoder & (idx == 0))
        def _():
            split_taps(0, 0, 9)
            reload_taps(0, 9)

        def one_slot(s, _):
            @pl.when((idx < 2 * ticks - 2) & went_early(idx))
            def _():
                @pl.when(s == 3)
                def _():
                    relay_own(idx + 1)

                @pl.when(s == 4)
                def _():
                    relay_others(idx + 1)

            e, part = event_of(jnp.maximum(s - 1, 0))
            gathers = active & (s >= 1) & (s <= 2 * others)

            @pl.when(gathers & (part == 0))
            def _():
                q = source_of(e)
                for u in range(OWN_UNITS):
                    arrived(k, q, u)

                    @pl.when(jnp.logical_not(skip_held))
                    def _():
                        onward(k, q, u, False)

                    @pl.when(lends & (e < others - 1))
                    def _():
                        across(k, q, u).start()
                    swap_after(k, q, u)

            @pl.when(gathers & (part == 1))
            def _():
                q = source_of(e)
                for u in range(OWN_UNITS, UNITS):
                    @pl.when(jnp.logical_not(skip_held & twin_holds(q)))
                    def _():
                        arrived(k, q, u)

                    @pl.when(lends & (e < others - 1) & jnp.logical_not(twin_holds(q)))
                    def _():
                        across(k, q, u).start()

                    @pl.when((decoder & jnp.logical_not(skip_held)) | (encoder & solo))
                    def _():
                        onward(k, q, u, False)
                    swap_after(k, q, u)

            @pl.when(
                encoder & (kind == 1) & (t < ticks - 1) & ((seg == 0) | (t > 0))
                & (s == jnp.where(seg == 0, 2 * others - 1, slots - 1))
            )
            def _():
                for u in range(OWN_UNITS):
                    @pl.when(seg > 0)
                    def _():
                        arrived(k + 1, place, u)
                    send_near(k + 1, u, False)

            @pl.when(encoder & jnp.logical_not(local) & (s == 1))
            def _():
                for u in range(OWN_UNITS, UNITS):
                    arrived(k, place, u)
                    swap_after(k, place, u)

            @pl.when(encoder & (idx == 0) & (s >= 1) & (s < 4))
            def _():
                split_taps(1, 3 * s - 3, 3 * s)

            @pl.when((s >= third) & (s < third + 3))
            def _():
                low = 3 * (s - third)

                @pl.when(decoder & jnp.logical_not(merged) & (idx == 0))
                def _():
                    split_taps(0, low, low + 3)
                    reload_taps(low, low + 3)

                @pl.when(decoder & jnp.logical_not(merged) & (idx == 1))
                def _():
                    split_taps(1, low, low + 3)

                if merge:
                    @pl.when(merged & (idx == 0))
                    def _():
                        split_merged(low, low + 3)

            @pl.when(active)
            def _():
                i, h = event_of(jnp.maximum(s - 2, 0))
                q = jnp.where(s < 2, place, source_of(i))
                h = jnp.where(s < 2, s, h)

                for side in range(HALVES):
                    @pl.when(h == side)
                    def _():
                        for part, (low, _) in enumerate(PARTS):
                            if low // (UNITS // HALVES) == side:
                                swap(k, 1 - core, q, part).wait_recv()
                multiply(k, kind, q, h)
            return 0
        lax.fori_loop(0, slots, one_slot, 0)

        def after(start, rows_of):
            value = placed(start)

            def put(parts):
                @pl.when(t == ticks - 1)
                def _():
                    for c in range(CHUNKS):
                        out_ref[rows_of, cut_of(c)] = parts[c]

                @pl.when(t < ticks - 1)
                def _():
                    for c in range(CHUNKS):
                        passed_out[jnp.minimum(t, ticks - 2), rows_at(c, start, blk), :] = parts[c]

            @pl.when(encoder & (kind == 0))
            def _():
                result = silu(value)
                for c in range(CHUNKS):
                    g[k + 1, core, place, rows_at(c, start, blk), :] = result[:, cut_of(c)]

            @pl.when(encoder & (kind == 1))
            def _():
                put([
                    g[k - 1, core, place, rows_at(c, start, blk), :] + value[:, cut_of(c)]
                    for c in range(CHUNKS)
                ])

            @pl.when(decoder)
            def _():
                result = silu(value)
                put([result[:, cut_of(c)] for c in range(CHUNKS)])

        ends = active & ((kind == 1) | merged)

        @pl.when(encoder | ends)
        def _():
            over_rows(after)

        @pl.when(ends & (t < ticks - 1))
        def _():
            give_all(t, True)
        return 0

    def give(t, kind, u, count):
        into_encoder = seg + 1 < half
        slot = (
            jnp.where(into_encoder, encoder_slot(t + 1, 0), decoder_slot(t + 1, 0)),
            encoder_slot(t + 1, 0),
            decoder_slot(t + 1, 1),
        )[kind]
        target = (kept(seg + 1), kept(seg + 1 + half), segments - 1 - seg)[kind]
        return pltpu.make_async_remote_copy(
            src_ref=passed_out.at[t, units_of(u, count)],
            dst_ref=g.at[slot, core, place, units_of(u, count)],
            send_sem=pass_sem.at[t, kind],
            recv_sem=recv_sem.at[slot, place, u],
            device_id=(target, me),
            device_id_type=MESH,
        )

    def give_all(t, starting):
        next_in = (seg + 1 < half) | ((seg < segments - 1) & decoder_active(seg + 1, t + 1))
        helper = seg + 1 < half
        mirror = segments - 1 - seg
        skip = encoder & decoder_active(mirror, t + 1)
        if merge:
            skip = skip & (mirror != half)
        if (segments + half) % 2 == 0:
            skip = skip & (mirror != shared)
        mixed = sorted(range(UNITS), key=lambda u: (u % OWN_UNITS, u))
        if starting:
            @pl.when(helper)
            def _():
                for u in mixed:
                    give(t, 0 if u < OWN_UNITS else 1, u, 1).start()

            @pl.when(next_in & jnp.logical_not(helper))
            def _():
                for u in range(UNITS):
                    give(t, 0, u, 1).start()

            @pl.when(skip)
            def _():
                for u in range(UNITS):
                    give(t, 2, u, 1).start()
        else:
            @pl.when(helper)
            def _():
                give(t, 0, 0, OWN_UNITS).wait_send()
                give(t, 1, OWN_UNITS, UNITS - OWN_UNITS).wait_send()

            @pl.when(next_in & jnp.logical_not(helper))
            def _():
                give(t, 0, 0, UNITS).wait_send()

            @pl.when(skip)
            def _():
                give(t, 2, 0, UNITS).wait_send()

    lax.fori_loop(0, 2 * ticks, one_stage, 0)
    for idx in range(max(0, 2 * ticks - 2), 2 * ticks):
        drain(idx)

    for t in range(ticks - 1):
        @pl.when(encoder | decoder_active(seg, t))
        def _():
            give_all(t, False)


def body(segments, n, resident, held_skip, fresh, first_weight, second_weight):
    ticks = fresh.shape[0] + 1
    rows, positions = resident.shape[1:]
    length = n // 2
    width = 2 * rows
    slots = 2 * ticks + 2 * (ticks - first_decoder_tick(segments, ticks))
    vmem = pl.BlockSpec(memory_space=pltpu.VMEM)
    anywhere = pl.BlockSpec(memory_space=pl.ANY)
    out = pl.pallas_call(
        functools.partial(kernel, segments, n, ticks),
        out_shape=jax.ShapeDtypeStruct((rows, positions), jnp.float32),
        in_specs=[vmem, vmem, vmem, anywhere, anywhere],
        out_specs=vmem,
        scratch_shapes=[
            pltpu.VMEM((9, rows, length * width), jnp.float32),
            pltpu.VMEM((2, length, 9 * rows, 3 * width), jnp.bfloat16),
            pltpu.VMEM((slots, 2, length, CHUNKS * rows, positions // CHUNKS), jnp.float32),
            pltpu.VMEM((3 * width, positions // HALVES), jnp.bfloat16),
            pltpu.VMEM((HALVES, 9 * rows, positions // HALVES), jnp.float32),
            pltpu.VMEM((ticks - 1, CHUNKS * rows, positions // CHUNKS), jnp.float32),
            pltpu.SemaphoreType.DMA((9,)),
            pltpu.SemaphoreType.DMA((slots, length, UNITS)),
            pltpu.SemaphoreType.DMA((slots, length, len(PARTS))),
            pltpu.SemaphoreType.DMA((slots,)),
            pltpu.SemaphoreType.DMA((slots, 2, length)),
            pltpu.SemaphoreType.DMA((slots, length)),
            pltpu.SemaphoreType.DMA((ticks - 1, 3)),
        ],
        compiler_params=pltpu.CompilerParams(
            collective_id=0, has_side_effects=True, vmem_limit_bytes=63 * 1024 * 1024
        ),
    )(resident[0], held_skip[0], fresh, first_weight, second_weight)
    return out[None]


def solution(mesh):
    return jax.shard_map(
        functools.partial(body, mesh.shape["segment"], mesh.shape["chan"]),
        mesh=mesh,
        in_specs=(
            P("segment", "chan", None),
            P("segment", "chan", None),
            P(None, "chan", None),
            P("segment", "chan", None),
            P("segment", "chan", None),
        ),
        out_specs=P("segment", "chan", None),
        check_vma=False,
    )
```

```python
import functools

import jax
import jax.numpy as jnp
from jax import lax
from jax.experimental import pallas as pl
from jax.experimental.pallas import tpu as pltpu
from jax.sharding import PartitionSpec as P

ROWS = 16
COLS = 32
MESH = pl.DeviceIdType.MESH
HALVES = 2
PIECES = 2
CHUNKS = HALVES * PIECES
UNITS = 8
OWN_UNITS = 5
CUTS = sorted({0, UNITS // 2, OWN_UNITS, UNITS})
PARTS = tuple(zip(CUTS[:-1], CUTS[1:]))


def silu(v):
    return v / (1.0 + jnp.exp(-v))


def first_decoder_tick(segments, ticks):
    return max(0, ticks - segments // 2)


def kernel(
    segments, n, ticks,
    resident, held_skip, fresh, first_weight, second_weight, out_ref,
    stage, wv, g, operand, acc, passed_out,
    w_sem, recv_sem, swap_sem, partner_sem, z_sem, y_sem, pass_sem,
):
    seg = lax.axis_index("segment")
    me = lax.axis_index("chan")
    place = me // 2
    core = me % 2
    partner = me + 1 - 2 * core
    length = n // 2
    half = segments // 2
    encoder = seg < half
    decoder = jnp.logical_not(encoder)
    first_tick = first_decoder_tick(segments, ticks)
    merge = first_tick >= 1
    merged = (seg == half) & merge
    rows, positions = resident.shape
    part_positions = positions // HALVES
    piece = positions // CHUNKS
    width = 2 * rows
    channels = length * width
    blk = rows
    twin = jnp.where(encoder, seg + half, seg - half)

    def load(conv, tap, slot):
        source = (first_weight, second_weight)[conv]
        columns = pl.ds(pl.multiple_of(tap * channels, 128), channels)
        return pltpu.make_async_copy(source.at[0, :, columns], stage.at[slot], w_sem.at[slot])

    def store_split(conv, tap, value_of):
        spot = pl.ds(pl.multiple_of(tap * rows, 16 if rows % 16 == 0 else 8), rows)
        for q in range(length):
            value = value_of(slice(q * width, (q + 1) * width))
            high = value.astype(jnp.bfloat16)
            low = (value - high.astype(jnp.float32)).astype(jnp.bfloat16)
            wv[conv, q, spot, 0:width] = high
            wv[conv, q, spot, width : 2 * width] = low
            wv[conv, q, spot, 2 * width : 3 * width] = high

    depth = 4

    def start_first_loads():
        @pl.when(jnp.logical_not(merged))
        def _():
            def one(tap, _):
                load(0, tap, tap).start()
                return 0
            lax.fori_loop(0, 9, one, 0)

        if merge:
            @pl.when(merged)
            def _():
                for tap in range(depth):
                    load(0, tap, tap).start()
                    load(1, tap, depth + tap).start()

    def split_taps(conv, low, high):
        def one(tap, _):
            load(0, 0, tap).wait()
            store_split(conv, tap, lambda c: stage[tap, :, c])
            return 0
        lax.fori_loop(low, high, one, 0)

    def reload_taps(low, high):
        def one(tap, _):
            load(1, tap, tap).start()
            return 0
        lax.fori_loop(low, high, one, 0)

    def split_merged(low, high):
        def one(tap, _):
            a = tap % depth
            load(0, 0, a).wait()
            load(1, 0, depth + a).wait()
            store_split(0, tap, lambda c: stage[a, :, c] + stage[depth + a, :, c])

            @pl.when(tap + depth < 9)
            def _():
                load(0, tap + depth, a).start()
                load(1, tap + depth, depth + a).start()
            return 0
        lax.fori_loop(low, high, one, 0)

    start_first_loads()

    barrier = pltpu.get_barrier_semaphore()

    def greet(cond, segment, chan):
        @pl.when(cond)
        def _():
            pl.semaphore_signal(barrier, inc=1, device_id=(segment, chan), device_id_type=MESH)
        return jnp.where(cond, 1, 0)

    def kept(s):
        return jnp.clip(s, 0, segments - 1)

    greeted = greet(seg >= 0, seg, partner)
    for p in range(length):
        greeted += greet(place != p, seg, 2 * p + core)
        greeted += greet(seg >= 0, twin, 2 * p + core)
    greeted += greet(seg > 0, kept(seg - 1), me)
    greeted += greet(seg < segments - 1, kept(seg + 1), me)
    greeted += greet(seg >= 0, segments - 1 - seg, me)
    greeted += greet(seg + 1 < half, kept(seg + 1 + half), me)
    greeted += greet(seg >= half + 1, kept(seg - 1 - half), me)

    def encoder_slot(t, kind):
        return 2 * t + kind

    def decoder_slot(t, kind):
        return 2 * ticks + 2 * jnp.maximum(t - first_tick, 0) + kind

    def decoder_active(s, t):
        return s + (ticks - 1 - t) <= segments - 1

    shared = (segments + half) // 2
    shares = seg == shared
    if (segments + half) % 2:
        shares = seg < 0

    unit = CHUNKS * rows // UNITS

    def units_of(u, count):
        return pl.ds(u * unit, count * unit)

    def copy(k, q, u, count, sem, target_seg, target):
        return pltpu.make_async_remote_copy(
            src_ref=g.at[k, core, q, units_of(u, count)],
            dst_ref=g.at[k, core, q, units_of(u, count)],
            send_sem=sem,
            recv_sem=recv_sem.at[k, q, u],
            device_id=(target_seg, target),
            device_id_type=MESH,
        )

    def swap(k, parity, q, part):
        low, high = PARTS[part]
        return pltpu.make_async_remote_copy(
            src_ref=g.at[k, parity, q, units_of(low, high - low)],
            dst_ref=g.at[k, parity, q, units_of(low, high - low)],
            send_sem=partner_sem.at[k],
            recv_sem=swap_sem.at[k, q, part],
            device_id=(seg, partner),
            device_id_type=MESH,
        )

    def across(k, q, u):
        return copy(k, q, u, 1, y_sem.at[k, q], twin, me)

    def arrived(k, q, u):
        copy(k, q, u, 1, y_sem.at[k, q], twin, me).wait_recv()

    near = jnp.minimum(place, length - 1 - place)
    at_end = near == 0
    inner = jnp.where(place < length // 2, 1, -1)

    def along(k, q, u, lane, target, relay):
        target = jnp.clip(target, 0, length - 1)
        ending = (target == 0) | (target == length - 1)
        to = jnp.where(relay & (at_end | ending), twin, seg)
        return copy(k, q, u, 1, z_sem.at[k, lane, q], to, 2 * target + core)

    def send_near(k, u, relay):
        along(k, place, u, 0, place + inner, relay).start()

        @pl.when(jnp.logical_not(at_end))
        def _():
            along(k, place, u, 1, place - inner, relay).start()

    def send_far(k):
        @pl.when(at_end)
        def _():
            for d in range(2, length):
                for u in range(OWN_UNITS, UNITS):
                    along(k, place, u, 1, place + inner * d, True).start()

    def twin_holds(q):
        return (q > 0) & (q < length - 1) & jnp.logical_not(at_end)

    def onward(k, q, u, relay):
        @pl.when(twin_holds(q) if relay else jnp.logical_not(at_end))
        def _():
            along(k, q, u, 0, place + jnp.where(q < place, 1, -1), relay).start()

    def swap_after(k, q, u):
        for part, (low, high) in enumerate(PARTS):
            if u == high - 1:
                swap(k, core, q, part).start()

    def source_of(i):
        paired = i < 2 * near
        d = jnp.where(paired, i // 2 + 1, i - near + 1)
        way = jnp.where(paired & (i % 2 == 1), -inner, inner)
        return place + way * d

    def multiply(k, w, q, h):
        for i in range(2):
            for p in range(PIECES):
                part = g[k, i, q, pl.ds((PIECES * h + p) * rows, rows)]
                high = part.astype(jnp.bfloat16)
                low = (part - high.astype(jnp.float32)).astype(jnp.bfloat16)
                cut = slice(p * piece, (p + 1) * piece)
                operand[i * rows : (i + 1) * rows, cut] = high
                operand[width + i * rows : width + (i + 1) * rows, cut] = high
                operand[2 * width + i * rows : 2 * width + (i + 1) * rows, cut] = low
        acc[h] += jnp.dot(wv[w, q], operand[...], preferred_element_type=jnp.float32)

    spot = lax.broadcasted_iota(jnp.int32, (blk, positions), 1)
    column = spot % COLS

    def placed(start):
        total = None
        for dx in (-1, 0, 1):
            column_sum = None
            for dy in (-1, 0, 1):
                tap = 3 * (dy + 1) + dx + 1
                at = pl.ds(pl.multiple_of(tap * rows + start, 8), blk)
                part = jnp.concatenate([acc[h, at, :] for h in range(HALVES)], axis=1)
                if dy:
                    part = pltpu.roll(part, (-dy * COLS) % positions, 1)
                    source = spot + dy * COLS
                    part = jnp.where((source >= 0) & (source < positions), part, 0.0)
                column_sum = part if column_sum is None else column_sum + part
            if dx:
                column_sum = pltpu.roll(column_sum, (-dx) % positions, 1)
                source = column + dx
                column_sum = jnp.where((source >= 0) & (source < COLS), column_sum, 0.0)
            total = column_sum if total is None else total + column_sum
        return total

    def over_rows(action):
        def one(i, _):
            start = pl.multiple_of(i * blk, 8)
            action(start, pl.ds(start, blk))
            return 0
        lax.fori_loop(0, rows // blk, one, 0)

    def cut_of(c):
        return slice(c * piece, (c + 1) * piece)

    def rows_at(c, start=0, count=None):
        return pl.ds(c * rows + start, rows if count is None else count)

    def fill(k, source):
        for c in range(CHUNKS):
            g[k, core, place, rows_at(c)] = source[:, cut_of(c)]

    @pl.when(encoder)
    def _():
        fill(0, resident)

    if first_tick == 0:
        @pl.when(decoder)
        def _():
            fill(2 * ticks, resident)
            fill(2 * ticks + 1, held_skip)

    @pl.when((seg == 0) | (seg == half))
    def _():
        for t in range(1, ticks):
            fill(2 * t, fresh.at[t - 1])

    pl.semaphore_wait(barrier, greeted)

    def drain_along(k, low, high, relay):
        def sent(q, lane):
            copy(k, q, low, high - low, z_sem.at[k, lane, q], seg, partner).wait_send()

        sent(place, 0)

        @pl.when(at_end & relay)
        def _():
            if length > 2:
                span = g.at[k, core, pl.ds(0, length - 2), units_of(low, high - low)]
                pltpu.make_async_remote_copy(
                    src_ref=span, dst_ref=span,
                    send_sem=z_sem.at[k, 1, place], recv_sem=recv_sem.at[k, 0, 0],
                    device_id=(seg, partner), device_id_type=MESH,
                ).wait_send()

        @pl.when(jnp.logical_not(at_end))
        def _():
            sent(place, 1)

            def one(q, _):
                @pl.when(q != place)
                def _():
                    sent(q, 0)
                return 0
            lax.fori_loop(int(relay), length - int(relay), one, 0)

    def drain_partner(k):
        pltpu.make_async_remote_copy(
            src_ref=g.at[k, core], dst_ref=g.at[k, core],
            send_sem=partner_sem.at[k], recv_sem=swap_sem.at[k, 0, 0],
            device_id=(seg, partner), device_id_type=MESH,
        ).wait_send()

    def drain_across(k, q, low, high):
        copy(k, q, low, high - low, y_sem.at[k, q], twin, me).wait_send()

    twin_of = jnp.where(encoder, seg, twin)

    def facts_of(idx):
        t = idx // 2
        kind = idx % 2
        skip_held = shares & (kind == 1) & (t > 0)
        k = jnp.where(
            encoder,
            encoder_slot(t, kind),
            jnp.where(skip_held, encoder_slot(t, 0), decoder_slot(t, kind)),
        )
        active = encoder | (decoder_active(seg, t) & jnp.logical_not(merged & (kind == 1)))
        solo = (twin_of == 0) & (idx == 2 * ticks - 1)
        lifts = encoder & ((kind == 1) | (t == 0)) & jnp.logical_not(solo)
        lends = encoder & (twin == shared) & (kind == 0) & (t > 0) & decoder_active(twin, t)
        if (segments + half) % 2:
            lends = lends & (seg < 0)
        return t, kind, k, active, lifts, lends, solo, skip_held

    def drain(idx):
        t, kind, k, active, lifts, lends, solo, skip_held = facts_of(idx)
        relayed = encoder_slot(t, kind)

        @pl.when(active)
        def _():
            drain_partner(k)

            @pl.when(encoder & jnp.logical_not(solo))
            def _():
                drain_along(k, 0, OWN_UNITS, False)

                @pl.when(lifts)
                def _():
                    drain_across(k, place, OWN_UNITS, UNITS)

                @pl.when(lends)
                def _():
                    def one(q, _):
                        partly = (q == place) | twin_holds(q)

                        @pl.when(partly)
                        def _():
                            drain_across(k, q, 0, OWN_UNITS)

                        @pl.when(jnp.logical_not(partly))
                        def _():
                            drain_across(k, q, 0, UNITS)
                        return 0
                    lax.fori_loop(0, length, one, 0)

            @pl.when((decoder & jnp.logical_not(skip_held)) | (encoder & solo))
            def _():
                drain_along(k, 0, UNITS, False)

        @pl.when(decoder & jnp.logical_not(solo))
        def _():
            drain_along(relayed, OWN_UNITS, UNITS, True)

            @pl.when((seg != half) & (kind == 0) & (t > 0))
            def _():
                drain_across(relayed, place, OWN_UNITS, UNITS)

            @pl.when(jnp.logical_not(at_end))
            def _():
                def one(q, _):
                    @pl.when(q != place)
                    def _():
                        drain_across(relayed, q, OWN_UNITS, UNITS)
                    return 0
                lax.fori_loop(1, length - 1, one, 0)

    others = length - 1
    slots = 2 * length
    third = slots - 4

    def event_of(e):
        h = e // others
        m = (e + 1) // 2
        eh = jnp.where(e == 0, 0, jnp.where(e == 2 * others - 1, 1, (e + 1) % 2))
        ei = jnp.where(e == 0, 0, jnp.where(e % 2 == 1, jnp.minimum(m, others - 1), e // 2 - 1))
        return jnp.where(at_end, ei, e - h * others), jnp.where(at_end, eh, h)

    def went_early(idx):
        facts = facts_of(idx)
        return (seg == half) & facts[3] & jnp.logical_not(facts[-1])

    def relay_own(idx):
        t = idx // 2
        kind = idx % 2
        relayed = encoder_slot(t, kind)
        handed = (kind == 0) & (t > 0)
        for u in range(OWN_UNITS, UNITS):
            @pl.when(jnp.logical_not((seg == half) & handed))
            def _():
                arrived(relayed, place, u)

            @pl.when((seg != half) & handed)
            def _():
                across(relayed, place, u).start()
            send_near(relayed, u, True)
        send_far(relayed)

    def relay_others(idx):
        relayed = encoder_slot(idx // 2, idx % 2)

        def one(i, _):
            q = source_of(i)

            @pl.when(twin_holds(q))
            def _():
                for u in range(OWN_UNITS, UNITS):
                    arrived(relayed, q, u)
                    onward(relayed, q, u, True)
                    across(relayed, q, u).start()
            return 0
        lax.fori_loop(0, others, one, 0)

    def one_stage(idx, _):
        t, kind, k, active, lifts, lends, solo, skip_held = facts_of(idx)
        local = jnp.where(encoder, (kind == 1) | (t == 0) | (seg == 0), t == 0)
        ahead = encoder & (kind == 0) & (t > 0) & (seg == 0)

        @pl.when(decoder & jnp.logical_not(solo | ((idx > 0) & went_early(idx - 1))))
        def _():
            relay_own(idx)
            relay_others(idx)

        @pl.when(active)
        def _():
            for u in range(OWN_UNITS):
                @pl.when(jnp.logical_not(local | ahead))
                def _():
                    arrived(k, place, u)

                @pl.when(jnp.logical_not(ahead | skip_held))
                def _():
                    send_near(k, u, False)

                @pl.when(lends)
                def _():
                    across(k, place, u).start()
                swap_after(k, place, u)

            @pl.when(local | decoder)
            def _():
                for u in range(OWN_UNITS, UNITS):
                    @pl.when(jnp.logical_not(local | skip_held))
                    def _():
                        arrived(k, place, u)

                    @pl.when((decoder & jnp.logical_not(skip_held)) | (encoder & solo))
                    def _():
                        send_near(k, u, False)

                    @pl.when(lifts)
                    def _():
                        across(k, place, u).start()
                    swap_after(k, place, u)

            @pl.when(encoder & (kind == 1) & facts_of(jnp.maximum(idx - 1, 0))[5])
            def _():
                q = source_of(others - 1)
                for u in range(UNITS):
                    if u < OWN_UNITS:
                        across(k - 1, q, u).start()
                    else:
                        @pl.when(jnp.logical_not(twin_holds(q)))
                        def _():
                            across(k - 1, q, u).start()

            @pl.when(encoder | (kind == 0))
            def _():
                acc[...] = jnp.zeros_like(acc)

        @pl.when(idx > 1)
        def _():
            drain(idx - 2)

        @pl.when(encoder & (idx == 0))
        def _():
            split_taps(0, 0, 9)
            reload_taps(0, 9)

        def one_slot(s, _):
            @pl.when((idx < 2 * ticks - 2) & went_early(idx))
            def _():
                @pl.when(s == 3)
                def _():
                    relay_own(idx + 1)

                @pl.when(s == 4)
                def _():
                    relay_others(idx + 1)

            e, part = event_of(jnp.maximum(s - 1, 0))
            gathers = active & (s >= 1) & (s <= 2 * others)

            @pl.when(gathers & (part == 0))
            def _():
                q = source_of(e)
                for u in range(OWN_UNITS):
                    arrived(k, q, u)

                    @pl.when(jnp.logical_not(skip_held))
                    def _():
                        onward(k, q, u, False)

                    @pl.when(lends & (e < others - 1))
                    def _():
                        across(k, q, u).start()
                    swap_after(k, q, u)

            @pl.when(gathers & (part == 1))
            def _():
                q = source_of(e)
                for u in range(OWN_UNITS, UNITS):
                    @pl.when(jnp.logical_not(skip_held & twin_holds(q)))
                    def _():
                        arrived(k, q, u)

                    @pl.when(lends & (e < others - 1) & jnp.logical_not(twin_holds(q)))
                    def _():
                        across(k, q, u).start()

                    @pl.when((decoder & jnp.logical_not(skip_held)) | (encoder & solo))
                    def _():
                        onward(k, q, u, False)
                    swap_after(k, q, u)

            @pl.when(
                (seg == 0) & (kind == 1) & (t < ticks - 1) & (s == 2 * others - 1)
            )
            def _():
                for u in range(OWN_UNITS):
                    send_near(k + 1, u, False)

            @pl.when(encoder & jnp.logical_not(local) & (s == 1))
            def _():
                for u in range(OWN_UNITS, UNITS):
                    arrived(k, place, u)
                    swap_after(k, place, u)

            @pl.when(encoder & (idx == 0) & (s >= 1) & (s < 4))
            def _():
                split_taps(1, 3 * s - 3, 3 * s)

            @pl.when((s >= third) & (s < third + 3))
            def _():
                low = 3 * (s - third)

                @pl.when(decoder & jnp.logical_not(merged) & (idx == 0))
                def _():
                    split_taps(0, low, low + 3)
                    reload_taps(low, low + 3)

                @pl.when(decoder & jnp.logical_not(merged) & (idx == 1))
                def _():
                    split_taps(1, low, low + 3)

                if merge:
                    @pl.when(merged & (idx == 0))
                    def _():
                        split_merged(low, low + 3)

            @pl.when(active)
            def _():
                i, h = event_of(jnp.maximum(s - 2, 0))
                q = jnp.where(s < 2, place, source_of(i))
                h = jnp.where(s < 2, s, h)

                for side in range(HALVES):
                    @pl.when(h == side)
                    def _():
                        for part, (low, _) in enumerate(PARTS):
                            if low // (UNITS // HALVES) == side:
                                swap(k, 1 - core, q, part).wait_recv()
                multiply(k, kind, q, h)
            return 0
        lax.fori_loop(0, slots, one_slot, 0)

        def after(start, rows_of):
            value = placed(start)

            def put(parts):
                @pl.when(t == ticks - 1)
                def _():
                    for c in range(CHUNKS):
                        out_ref[rows_of, cut_of(c)] = parts[c]

                @pl.when(t < ticks - 1)
                def _():
                    for c in range(CHUNKS):
                        passed_out[jnp.minimum(t, ticks - 2), rows_at(c, start, blk), :] = parts[c]

            @pl.when(encoder & (kind == 0))
            def _():
                result = silu(value)
                for c in range(CHUNKS):
                    g[k + 1, core, place, rows_at(c, start, blk), :] = result[:, cut_of(c)]

            @pl.when(encoder & (kind == 1))
            def _():
                put([
                    g[k - 1, core, place, rows_at(c, start, blk), :] + value[:, cut_of(c)]
                    for c in range(CHUNKS)
                ])

            @pl.when(decoder)
            def _():
                result = silu(value)
                put([result[:, cut_of(c)] for c in range(CHUNKS)])

        ends = active & ((kind == 1) | merged)

        @pl.when(encoder | ends)
        def _():
            over_rows(after)

        @pl.when(ends & (t < ticks - 1))
        def _():
            give_all(t, True)
        return 0

    def give(t, kind, u, count):
        into_encoder = seg + 1 < half
        slot = (
            jnp.where(into_encoder, encoder_slot(t + 1, 0), decoder_slot(t + 1, 0)),
            encoder_slot(t + 1, 0),
            decoder_slot(t + 1, 1),
        )[kind]
        target = (kept(seg + 1), kept(seg + 1 + half), segments - 1 - seg)[kind]
        return pltpu.make_async_remote_copy(
            src_ref=passed_out.at[t, units_of(u, count)],
            dst_ref=g.at[slot, core, place, units_of(u, count)],
            send_sem=pass_sem.at[t, kind],
            recv_sem=recv_sem.at[slot, place, u],
            device_id=(target, me),
            device_id_type=MESH,
        )

    def give_all(t, starting):
        next_in = (seg + 1 < half) | ((seg < segments - 1) & decoder_active(seg + 1, t + 1))
        helper = seg + 1 < half
        mirror = segments - 1 - seg
        skip = encoder & decoder_active(mirror, t + 1)
        if merge:
            skip = skip & (mirror != half)
        if (segments + half) % 2 == 0:
            skip = skip & (mirror != shared)
        mixed = sorted(range(UNITS), key=lambda u: (u % OWN_UNITS, u))
        if starting:
            @pl.when(helper)
            def _():
                for u in mixed:
                    give(t, 0 if u < OWN_UNITS else 1, u, 1).start()

            @pl.when(next_in & jnp.logical_not(helper))
            def _():
                for u in range(UNITS):
                    give(t, 0, u, 1).start()

            @pl.when(skip)
            def _():
                for u in range(UNITS):
                    give(t, 2, u, 1).start()
        else:
            @pl.when(helper)
            def _():
                give(t, 0, 0, OWN_UNITS).wait_send()
                give(t, 1, OWN_UNITS, UNITS - OWN_UNITS).wait_send()

            @pl.when(next_in & jnp.logical_not(helper))
            def _():
                give(t, 0, 0, UNITS).wait_send()

            @pl.when(skip)
            def _():
                give(t, 2, 0, UNITS).wait_send()

    lax.fori_loop(0, 2 * ticks, one_stage, 0)
    for idx in range(max(0, 2 * ticks - 2), 2 * ticks):
        drain(idx)

    for t in range(ticks - 1):
        @pl.when(encoder | decoder_active(seg, t))
        def _():
            give_all(t, False)


def body(segments, n, resident, held_skip, fresh, first_weight, second_weight):
    ticks = fresh.shape[0] + 1
    rows, positions = resident.shape[1:]
    length = n // 2
    width = 2 * rows
    slots = 2 * ticks + 2 * (ticks - first_decoder_tick(segments, ticks))
    vmem = pl.BlockSpec(memory_space=pltpu.VMEM)
    anywhere = pl.BlockSpec(memory_space=pl.ANY)
    out = pl.pallas_call(
        functools.partial(kernel, segments, n, ticks),
        out_shape=jax.ShapeDtypeStruct((rows, positions), jnp.float32),
        in_specs=[vmem, vmem, vmem, anywhere, anywhere],
        out_specs=vmem,
        scratch_shapes=[
            pltpu.VMEM((9, rows, length * width), jnp.float32),
            pltpu.VMEM((2, length, 9 * rows, 3 * width), jnp.bfloat16),
            pltpu.VMEM((slots, 2, length, CHUNKS * rows, positions // CHUNKS), jnp.float32),
            pltpu.VMEM((3 * width, positions // HALVES), jnp.bfloat16),
            pltpu.VMEM((HALVES, 9 * rows, positions // HALVES), jnp.float32),
            pltpu.VMEM((ticks - 1, CHUNKS * rows, positions // CHUNKS), jnp.float32),
            pltpu.SemaphoreType.DMA((9,)),
            pltpu.SemaphoreType.DMA((slots, length, UNITS)),
            pltpu.SemaphoreType.DMA((slots, length, len(PARTS))),
            pltpu.SemaphoreType.DMA((slots,)),
            pltpu.SemaphoreType.DMA((slots, 2, length)),
            pltpu.SemaphoreType.DMA((slots, length)),
            pltpu.SemaphoreType.DMA((ticks - 1, 3)),
        ],
        compiler_params=pltpu.CompilerParams(
            collective_id=0, has_side_effects=True, vmem_limit_bytes=63 * 1024 * 1024
        ),
    )(resident[0], held_skip[0], fresh, first_weight, second_weight)
    return out[None]


def solution(mesh):
    return jax.shard_map(
        functools.partial(body, mesh.shape["segment"], mesh.shape["chan"]),
        mesh=mesh,
        in_specs=(
            P("segment", "chan", None),
            P("segment", "chan", None),
            P(None, "chan", None),
            P("segment", "chan", None),
            P("segment", "chan", None),
        ),
        out_specs=P("segment", "chan", None),
        check_vma=False,
    )
```
